512 devices in a mesh: dp: 8 (over x, core), ctx: 64 (over y, z).
Axes of the slice: x: 4, y: 4, z: 16, core: 2. Of those that a mesh axis runs over, the one named last changes fastest.
Arguments:
- peak_rows: bfloat16 [8, 16384, 1024], P('dp', 'ctx'), may hold values from -6 to 6
- row_route: int32 [8, 16384], P('dp', 'ctx'), may hold values from -1 to 7, as said below
- inducing: bfloat16 [256, 1024], replicated, may hold values from -320 to 320
- w_key: bfloat16 [1024, 1024], P('ctx'), may hold values from -0.1875 to 0.1875
- w_value: bfloat16 [1024, 1024], P('ctx'), may hold values from -0.1875 to 0.1875
- w_query: bfloat16 [1024, 1024], P('ctx'), may hold values from -0.1875 to 0.1875
Outputs:
- summary: bfloat16 [8, 256, 1024], P('dp')
- local_queries: bfloat16 [8, 16384, 1024], P('dp', 'ctx')
- moved_queries: bfloat16 [8, 8192, 1024], P('dp', 'ctx')
The draws below stay inside these ranges and needn't reach their ends.
Inputs may be any that keep to these rules, and one draw needn't show every extreme that they name: `row_route`: in each set the live rows (route 0 or more) are its first rows and the rest are -1; every set has 256 or more live rows and one set has all 16384. A live row's route is its own set's index or another set's index. Among the 256 rows of one device at most 144 keep their own set's index and at most 16 name any one other set; a device whose rows are all live keeps exactly 144 and names every other set exactly 16 times.
All inputs are finite; a program needn't handle non-finite values.
Results may differ from the reference program's by a relative error of at most 0.00705.
The reference program's roundings to bfloat16 on the way (of `keys`, `values`, `queries` and `probs`) count: a program that leaves them out, or rounds other values in their place, can miss the bound.
Values may be sent and summed in bfloat16 or wider, within the bound.
A program may use at most 64 MiB of HBM per device.

```python
import math
import jax
import jax.numpy as jnp
from jax import lax

D = 1024
HEADS = 8
INDUCING = 256
ROWS = 256
CAP = 16
KEEP = 144
SETS = 8
SET_ROWS = 16384


def draw_row_route(key, part):
    ctx_count = SET_ROWS // ROWS
    key_len, key_full, key_order, key_shift = jax.random.split(key, 4)
    lengths = jax.random.randint(key_len, (SETS,), ROWS, SET_ROWS + 1)
    full_set = jax.random.randint(key_full, (), 0, SETS)
    lengths = jnp.where(jnp.arange(SETS) == full_set, SET_ROWS, lengths)
    starts = jnp.arange(ctx_count, dtype=jnp.int32) * ROWS
    live_count = jnp.clip(lengths[:, None] - starts[None, :], 0, ROWS)
    excess = jnp.maximum(live_count - KEEP, 0)
    row_ids = jnp.arange(ROWS, dtype=jnp.int32)
    priority = jax.random.randint(key_order, (SETS, ctx_count, ROWS), 0, 2 ** 16) * ROWS + row_ids
    is_live = row_ids[None, None, :] < live_count[:, :, None]
    ranking_score = jnp.where(is_live, priority, 2 ** 28 + row_ids)
    order = jnp.argsort(ranking_score, axis=-1, stable=True)
    rank = jnp.argsort(order, axis=-1, stable=True).astype(jnp.int32)
    moved = rank < excess[:, :, None]
    shift = jax.random.randint(key_shift, (SETS, ctx_count, 1), 0, SETS - 1)
    own_group = jnp.arange(SETS, dtype=jnp.int32)[:, None, None]
    dest_group = (own_group + 1 + (rank + shift) % (SETS - 1)) % SETS
    route = jnp.where(is_live, jnp.where(moved, dest_group, own_group), -1)
    return route.reshape(SETS, SET_ROWS).astype(jnp.int32)


def draw_inducing(key, part):
    base = jax.random.truncated_normal(key, -5.0, 5.0, (INDUCING, D), jnp.float32)
    return base.astype(jnp.bfloat16)


def block_scale(stream_key, shape, shards, least, top_value):
    def one(axis_at, parts):
        heights = jax.random.uniform(jax.random.fold_in(jax.random.fold_in(stream_key, 6), axis_at), (parts,), jnp.float32, least / len(shards), top_value / len(shards))
        return jnp.repeat(jnp.exp(heights), shape[axis_at] // parts).reshape((-1,) + (1,) * (len(shape) - axis_at - 1))

    gain = one(*shards[0])
    for cut in shards[1:]:
        gain = gain * one(*cut)
    return gain


def bell_draw(key, shape, spread, most, shards=(), kind=jnp.bfloat16):
    level = block_scale(key, shape, shards, -0.22, 0.18) if shards else 1.0
    result = jax.random.normal(key, shape, jnp.float32) * spread * level
    return jnp.minimum(jnp.maximum(result, -most), most).astype(kind)


def setup_inputs(seed: int = 0) -> dict:
    arg_keys = jax.random.split(jax.random.key(seed), 7)
    peak_rows = bell_draw(arg_keys[0], (SETS, SET_ROWS, D), 1.0, 6.0, ((0, 8), (1, 64)))
    row_route = draw_row_route(jax.random.fold_in(arg_keys[6], 71), 0)
    inducing = draw_inducing(jax.random.fold_in(arg_keys[6], 71), 0)
    w_key = bell_draw(arg_keys[3], (D, D), D ** -0.5, 0.1875, ((0, 64),))
    w_value = bell_draw(arg_keys[4], (D, D), D ** -0.5, 0.1875, ((0, 64),))
    w_query = bell_draw(arg_keys[5], (D, D), D ** -0.5, 0.1875, ((0, 64),))
    return dict(peak_rows=peak_rows, row_route=row_route, inducing=inducing, w_key=w_key, w_value=w_value, w_query=w_query)


def reference(peak_rows, row_route, inducing, w_key, w_value, w_query):
    sets = peak_rows.shape[0]
    set_rows = peak_rows.shape[1]
    width = peak_rows.shape[2]
    head_size = width // HEADS
    point_count = inducing.shape[0]
    ctx_count = set_rows // ROWS
    query_heads = inducing.astype(jnp.float32).reshape(point_count, HEADS, head_size)

    def per_set(operands):
        rows_in, routes, set_index = operands
        keys = lax.optimization_barrier(jnp.dot(rows_in, w_key, preferred_element_type=jnp.float32).astype(jnp.bfloat16))
        values = lax.optimization_barrier(jnp.dot(rows_in, w_value, preferred_element_type=jnp.float32).astype(jnp.bfloat16))
        queries = jnp.dot(rows_in, w_query, preferred_element_type=jnp.float32).astype(jnp.bfloat16)
        live = routes >= 0
        key_heads = keys.astype(jnp.float32).reshape(set_rows, HEADS, head_size)
        value_heads = values.astype(jnp.float32).reshape(set_rows, HEADS, head_size)
        scores = jnp.einsum('mhe,nhe->hmn', query_heads, key_heads) / math.sqrt(head_size)
        scores = jnp.where(live[None, None, :], scores, jnp.float32(-1e+30))
        top_score = lax.optimization_barrier(jnp.max(scores, axis=2))
        exp_terms = jnp.where(live[None, None, :], jnp.exp(scores - top_score[:, :, None]), jnp.float32(0.0))
        totals = lax.optimization_barrier(jnp.sum(exp_terms, axis=2))
        probs = lax.optimization_barrier(exp_terms.astype(jnp.bfloat16)).astype(jnp.float32)
        weighted = jnp.einsum('hmn,nhe->hme', probs, value_heads)
        summary = (weighted / totals[:, :, None]).transpose(1, 0, 2).reshape(point_count, width).astype(jnp.bfloat16)
        local = jnp.where((routes == set_index)[:, None], queries, jnp.zeros_like(queries))
        return (summary, local, queries)
    summary, local_queries, queries = lax.map(per_set, (peak_rows, row_route, jnp.arange(sets, dtype=jnp.int32)))
    routes = row_route.reshape(sets, ctx_count, ROWS)
    targets = jnp.arange(sets, dtype=jnp.int32)
    own_group = jnp.arange(sets, dtype=jnp.int32)[:, None, None]
    outgoing = (routes[..., None] == targets) & (targets != own_group[..., None])
    send_slot = jnp.cumsum(outgoing.astype(jnp.int32), axis=2) - 1
    moved = (routes >= 0) & (routes != own_group)
    dest_group = jnp.clip(routes, 0, sets - 1).astype(jnp.int32)
    row_slot = jnp.take_along_axis(send_slot, dest_group[..., None], axis=3)[..., 0]
    ctx_ids = jnp.arange(ctx_count, dtype=jnp.int32)[None, :, None]
    total_slots = sets * ctx_count * sets * CAP
    flat_slot = jnp.where(moved, ((dest_group * ctx_count + ctx_ids) * sets + own_group) * CAP + row_slot, total_slots).astype(jnp.int32)
    moved_queries = jnp.zeros((total_slots, width), jnp.bfloat16).at[flat_slot.reshape(-1)].set(queries.reshape(-1, width), mode='drop')
    moved_queries = moved_queries.reshape(sets, ctx_count * sets * CAP, width)
    return (summary, local_queries, moved_queries)
```

```python
import math

import jax
import jax.numpy as jnp
from jax import lax
from jax.experimental import pallas as pl
from jax.experimental.pallas import tpu as pltpu
from jax.sharding import PartitionSpec as P

HEADS = 8
NY = 4
NZ = 16
HALF = NZ // 2
SCORE_FLOOR = -1e30
MESH = pl.DeviceIdType.MESH
VMEM = pl.BlockSpec(memory_space=pltpu.VMEM)


def place():
    dp = lax.axis_index("dp")
    ctx = lax.axis_index("ctx")
    return dp, lax.div(ctx, NZ), lax.rem(ctx, NZ)


def wrap(value, size):
    return lax.rem(value + size, size)


def remote(src, dst, send_sem, recv_sem, dp, y, z):
    return pltpu.make_async_remote_copy(
        src_ref=src,
        dst_ref=dst,
        send_sem=send_sem,
        recv_sem=recv_sem,
        device_id=(dp, y * NZ + z),
        device_id_type=MESH,
    )


def greet(partners):
    barrier = pltpu.get_barrier_semaphore()
    for dp, y, z in partners:
        pl.semaphore_signal(barrier, inc=1, device_id=(dp, y * NZ + z), device_id_type=MESH)
    pl.semaphore_wait(barrier, len(partners))


def gather_kernel(
    wk, wv, wq, kv, qf,
    local_sem, zas, zar, zqs, zqr, ys, yr, fs, fr, qs, qr, pas, par, pqs, pqr,
):
    dp, y, z = place()
    core = lax.rem(dp, 2)
    partner = dp + 1 - 2 * core
    width = wk.shape[1] // 2
    cols = pl.ds(pl.multiple_of(core * width, width), width)
    other = pl.ds(pl.multiple_of((1 - core) * width, width), width)

    def shifted(step, way):
        return wrap(z - step if way == 0 else z + step, NZ)

    def kv_ring(step, way, arriving):
        block = kv.at[:, y, shifted(step + 1 if arriving else step, way), :, cols]
        target = wrap(z + 1 if way == 0 else z - 1, NZ)
        return remote(block, block, zas.at[way, step], zar.at[way, step], dp, y, target)

    def q_ring(step, way, arriving):
        block = qf.at[:, shifted(step + 1 if arriving else step, way), :, cols]
        target = wrap(z + 1 if way == 0 else z - 1, NZ)
        return remote(block, block, zqs.at[way, step], zqr.at[way, step], dp, y, target)

    def kv_side(step, way, side, arriving):
        row = y if not arriving else wrap(y - 1 if side == 0 else y + 1, NY)
        block = kv.at[:, row, shifted(step, way), :, cols]
        slot = 2 * step + way
        target = wrap(y + 1 if side == 0 else y - 1, NY)
        return remote(block, block, ys.at[side, slot], yr.at[side, slot], dp, target, z)

    def kv_pass(step, way, side, arriving):
        hops = 2 if arriving else 1
        row = wrap(y - hops if side == 0 else y + hops, NY)
        block = kv.at[side, row, shifted(step, way), :, cols]
        slot = 2 * step + way
        target = wrap(y + 1 if side == 0 else y - 1, NY)
        return remote(block, block, fs.at[side, slot], fr.at[side, slot], dp, target, z)

    def kv_swap(step, way, arriving):
        block = kv.at[:, :, shifted(step, way), :, other if arriving else cols]
        slot = 2 * step + way
        return remote(block, block, pas.at[slot], par.at[slot], partner, y, z)

    def q_swap(step, way, arriving):
        block = qf.at[:, shifted(step, way), :, other if arriving else cols]
        slot = 2 * step + way
        return remote(block, block, pqs.at[slot], pqr.at[slot], partner, y, z)

    def q_side(hop, arriving):
        row = wrap(y - hop, NY) if arriving else y
        block = qf.at[row, z, :, cols]
        return remote(block, block, qs.at[hop - 1], qr.at[hop - 1], dp, wrap(y + hop, NY), z)

    def stage_kv(step, ways, onward):
        for way in ways:
            if not (isinstance(step, int) and step == 0):
                kv_ring(step - 1, way, True).wait_recv()
        for way in onward:
            kv_ring(step, way, False).start()
        for way in ways:
            for side in (0, 1):
                kv_side(step, way, side, False).start()

    def stage_q(step, ways, onward):
        for way in ways:
            if not (isinstance(step, int) and step == 0):
                q_ring(step - 1, way, True).wait_recv()
        for way in onward:
            q_ring(step, way, False).start()
        for way in ways:
            q_swap(step, way, False).start()

    def stage_pass(step, ways):
        for way in ways:
            for side in (0, 1):
                kv_side(step, way, side, True).wait_recv()
                kv_pass(step, way, side, False).start()

    def stage_swap(step, ways):
        for way in ways:
            for side in (0, 1):
                kv_pass(step, way, side, True).wait_recv()
            kv_swap(step, way, False).start()

    own = [
        pltpu.make_async_copy(wk.at[:, cols], kv.at[0, y, z, :, cols], local_sem.at[0]),
        pltpu.make_async_copy(wv.at[:, cols], kv.at[1, y, z, :, cols], local_sem.at[1]),
        pltpu.make_async_copy(wq.at[:, cols], qf.at[y, z, :, cols], local_sem.at[2]),
    ]
    for copy in own:
        copy.start()
    greet(
        [
            (dp, y, wrap(z + 1, NZ)),
            (dp, y, wrap(z - 1, NZ)),
            (dp, wrap(y + 1, NY), z),
            (dp, wrap(y + 2, NY), z),
            (dp, wrap(y + 3, NY), z),
            (partner, y, z),
        ]
    )
    for copy in own:
        copy.wait()

    both = (0, 1)
    for hop in (1, 3, 2):
        q_side(hop, False).start()
    stage_kv(0, (0,), both)
    for hop in (1, 3, 2):
        q_side(hop, True).wait_recv()
    stage_q(0, (0,), both)
    stage_kv(1, both, both)
    stage_q(1, both, both)
    stage_pass(0, (0,))

    def body(step, carry):
        stage_kv(step, both, both)
        stage_q(step, both, both)
        stage_pass(step - 1, both)

        @pl.when(step > 2)
        def _():
            stage_swap(step - 2, both)

        @pl.when(step == 2)
        def _():
            stage_swap(0, (0,))

        return carry

    lax.fori_loop(2, HALF - 1, body, 0)
    last = HALF - 1
    stage_kv(last, both, (0,))
    stage_q(last, both, (0,))
    stage_pass(last - 1, both)
    stage_swap(last - 2, both)
    stage_kv(HALF, (0,), ())
    stage_q(HALF, (0,), ())
    stage_pass(last, both)
    stage_swap(last - 1, both)
    stage_pass(HALF, (0,))
    stage_swap(last, both)
    stage_swap(HALF, (0,))

    for hop in (1, 2, 3):
        q_side(hop, False).wait_send()

    def finish_slot(step, ways):
        for way in ways:
            kv_swap(step, way, True).wait_recv()
            q_swap(step, way, True).wait_recv()
            kv_swap(step, way, False).wait_send()
            q_swap(step, way, False).wait_send()
            for side in (0, 1):
                kv_side(step, way, side, False).wait_send()
                kv_pass(step, way, side, False).wait_send()

    def finish_ring(step, ways):
        for way in ways:
            kv_ring(step, way, False).wait_send()
            q_ring(step, way, False).wait_send()

    finish_slot(0, (0,))
    finish_ring(0, both)

    def finish(step, carry):
        finish_slot(step, both)
        finish_ring(step, both)
        return carry

    lax.fori_loop(1, last, finish, 0)
    finish_slot(last, both)
    finish_ring(last, (0,))
    finish_slot(HALF, (0,))


def gather_weights(w_key, w_value, w_query):
    depth, width = w_key.shape
    dma = pltpu.SemaphoreType.DMA
    slots = 2 * HALF + 1
    kv, qf = pl.pallas_call(
        gather_kernel,
        out_shape=(
            jax.ShapeDtypeStruct((2, NY, NZ, depth, width), w_key.dtype),
            jax.ShapeDtypeStruct((NY, NZ, depth, width), w_key.dtype),
        ),
        in_specs=[VMEM] * 3,
        out_specs=(VMEM, VMEM),
        scratch_shapes=[
            dma((3,)),
            dma((2, HALF)), dma((2, HALF)),
            dma((2, HALF)), dma((2, HALF)),
            dma((2, slots)), dma((2, slots)),
            dma((2, slots)), dma((2, slots)),
            dma((3,)), dma((3,)),
            dma((slots,)), dma((slots,)),
            dma((slots,)), dma((slots,)),
        ],
        compiler_params=pltpu.CompilerParams(collective_id=0, has_side_effects=True),
        name="gather_weights",
    )(w_key, w_value, w_query)
    full = NY * NZ * depth
    return kv.reshape(2, full, width), qf.reshape(full, width)


def attend_kernel(rows, route_col, route_row, inducing, kv, qf, local_out, sent_out, part_out):
    own = lax.axis_index("dp")
    row_count, width = rows.shape
    groups = sent_out.shape[0] // 16
    points = inducing.shape[0]
    head_size = width // HEADS
    scale = jnp.float32(1.0 / math.sqrt(head_size))

    column = route_col[...]
    live = column >= 0
    keep = column == own

    lane_route = jnp.broadcast_to(route_row[...], (groups, row_count))
    target = lax.broadcasted_iota(jnp.int32, (groups, row_count), 0)
    outgoing = jnp.where((lane_route == target) & (target != own), 1.0, 0.0)
    before = lax.broadcasted_iota(jnp.int32, (row_count, row_count), 0)
    after = lax.broadcasted_iota(jnp.int32, (row_count, row_count), 1)
    ramp = jnp.where(before <= after, 1.0, 0.0).astype(jnp.bfloat16)
    rank = jnp.dot(outgoing.astype(jnp.bfloat16), ramp, preferred_element_type=jnp.float32)
    slot = lax.broadcasted_iota(jnp.int32, (16, row_count), 0).astype(jnp.float32) + 1.0
    picks = jnp.concatenate(
        [
            jnp.where(
                (jnp.broadcast_to(rank[g : g + 1], (16, row_count)) == slot)
                & (jnp.broadcast_to(outgoing[g : g + 1], (16, row_count)) > 0.5),
                1.0,
                0.0,
            )
            for g in range(groups)
        ],
        axis=0,
    ).astype(jnp.bfloat16)
    stat_row = lax.broadcasted_iota(jnp.int32, (8, points), 0)

    pair = 2 * head_size
    for block in range(width // pair):
        cols = pl.ds(block * pair, pair)
        keys = jnp.dot(rows[...], kv[0, :, cols], preferred_element_type=jnp.float32)
        keys = keys.astype(jnp.bfloat16)
        values = jnp.dot(rows[...], kv[1, :, cols], preferred_element_type=jnp.float32)
        values = values.astype(jnp.bfloat16)
        queries = jnp.dot(rows[...], qf[:, cols], preferred_element_type=jnp.float32)
        queries = queries.astype(jnp.bfloat16)
        local_out[:, cols] = jnp.where(keep, queries.astype(jnp.float32), 0.0).astype(jnp.bfloat16)
        sent_out[:, cols] = jnp.dot(
            picks, queries, preferred_element_type=jnp.float32
        ).astype(jnp.bfloat16)
        for sub in range(2):
            head = 2 * block + sub
            lanes = slice(sub * head_size, (sub + 1) * head_size)
            scores = lax.dot_general(
                keys[:, lanes],
                inducing[:, pl.ds(head * head_size, head_size)],
                (((1,), (1,)), ((), ())),
                preferred_element_type=jnp.float32,
            )
            scores = jnp.where(live, scores * scale, jnp.float32(SCORE_FLOOR))
            top = jnp.max(scores, axis=0, keepdims=True)
            terms = jnp.where(live, jnp.exp(scores - top), 0.0)
            total = jnp.sum(terms, axis=0, keepdims=True)
            weighted = lax.dot_general(
                values[:, lanes],
                terms.astype(jnp.bfloat16),
                (((0,), (0,)), ((), ())),
                preferred_element_type=jnp.float32,
            )
            part_out[head, 0:head_size, :] = weighted
            part_out[head, head_size : head_size + 8, :] = jnp.where(
                stat_row < 4,
                jnp.broadcast_to(top, (8, points)),
                jnp.broadcast_to(total, (8, points)),
            )


def attend(rows, route, inducing, kv, qf, groups):
    row_count, width = rows.shape
    points = inducing.shape[0]
    head_size = width // HEADS
    return pl.pallas_call(
        attend_kernel,
        out_shape=(
            jax.ShapeDtypeStruct((row_count, width), jnp.bfloat16),
            jax.ShapeDtypeStruct((groups * 16, width), jnp.bfloat16),
            jax.ShapeDtypeStruct((HEADS, head_size + 8, points), jnp.float32),
        ),
        in_specs=[VMEM] * 6,
        out_specs=(VMEM,) * 3,
        name="attend",
    )(rows, route.reshape(row_count, 1), route.reshape(1, row_count), inducing, kv, qf)


ORDER = (8, 7, 9, 6, 10, 5, 11, 4, 12, 3, 13, 2, 14, 1, 15)


def combine_kernel(
    part, sent, summary, moved,
    from_y, to_z, from_z, piece,
    local_sem, ms, mr, ys, yr, zs, zr, gs, gr, hs, hr,
):
    dp, y, z = place()
    groups = sent.shape[0]
    head_size = summary.shape[1]
    quarter = head_size // 4

    greet(
        [(wrap(dp + k, groups), y, z) for k in range(1, groups)]
        + [(dp, wrap(y + k, NY), z) for k in range(1, NY)]
        + [(dp, y, wrap(z + k, NZ)) for k in range(1, NZ)]
    )

    def swap_y(k):
        there = wrap(y + k, NY)
        return remote(
            part.at[pl.ds(2 * there, 2)], from_y.at[k - 1], ys.at[k - 1], yr.at[k - 1], dp, there, z
        )

    for k in (2, 1, 3):
        swap_y(k).start()

    def move(k, arriving):
        there = wrap(dp + k, groups)
        slot = wrap(dp - k, groups) if arriving else dp
        return remote(sent.at[there], moved.at[slot], ms.at[k - 1], mr.at[k - 1], there, y, z)

    for k in range(1, groups):
        move(k, False).start()
    keep_own = pltpu.make_async_copy(sent.at[dp], moved.at[dp], local_sem.at[0])
    keep_own.start()

    for k in range(1, NY):
        swap_y(k).wait_recv()

    stat_row = lax.broadcasted_iota(jnp.int32, (8, 128), 0)
    for head in range(2):
        for half in range(2):
            lanes = slice(half * 128, half * 128 + 128)
            sources = [part.at[2 * y + head]] + [from_y.at[k, head] for k in range(NY - 1)]
            tops = [s[head_size : head_size + 1, lanes] for s in sources]
            totals = [s[head_size + 4 : head_size + 5, lanes] for s in sources]
            top = tops[0]
            for other in tops[1:]:
                top = jnp.maximum(top, other)
            shares = [jnp.exp(t - top) for t in tops]
            total = totals[0] * shares[0]
            for other, share in zip(totals[1:], shares[1:]):
                total = total + other * share
            stats = jnp.where(
                stat_row < 4, jnp.broadcast_to(top, (8, 128)), jnp.broadcast_to(total, (8, 128))
            )
            for group in range(4):
                lines = slice(group * quarter, (group + 1) * quarter)
                value = sources[0][lines, lanes] * shares[0]
                for source, share in zip(sources[1:], shares[1:]):
                    value = value + source[lines, lanes] * share
                slot = head * 8 + half * 4 + group
                to_z[slot, 0:quarter, :] = value
                to_z[slot, quarter : quarter + 8, :] = stats

    def swap_z(k):
        there = wrap(z + k, NZ)
        return remote(
            to_z.at[there], from_z.at[k - 1], zs.at[k - 1], zr.at[k - 1], dp, y, there
        )

    for k in ORDER:
        swap_z(k).start()
    for k in reversed(ORDER):
        swap_z(k).wait_recv()

    sources = [to_z.at[z]] + [from_z.at[k] for k in range(NZ - 1)]
    tops = [s[quarter : quarter + 1, :] for s in sources]
    top = tops[0]
    for other in tops[1:]:
        top = jnp.maximum(top, other)
    value = None
    total = None
    for source, own_top in zip(sources, tops):
        share = jnp.exp(own_top - top)
        term = source[0:quarter, :] * share
        count = source[quarter + 4 : quarter + 5, :] * share
        value = term if value is None else value + term
        total = count if total is None else total + count
    piece[...] = (value / total).astype(jnp.bfloat16)

    def spot(there):
        return summary.at[
            2 * y + lax.div(there, 8),
            pl.ds(pl.multiple_of(lax.rem(there, 4) * quarter, quarter), quarter),
            pl.ds(pl.multiple_of(lax.rem(lax.div(there, 4), 2) * 128, 128), 128),
        ]

    def spread_z(k, arriving):
        owner = wrap(z - k, NZ) if arriving else z
        return remote(
            piece, spot(owner), gs.at[k - 1], gr.at[k - 1], dp, y, wrap(z + k, NZ)
        )

    for k in ORDER:
        spread_z(k, False).start()
    own_piece = pltpu.make_async_copy(piece, spot(z), local_sem.at[1])
    own_piece.start()
    own_piece.wait()
    for k in reversed(ORDER):
        spread_z(k, True).wait_recv()

    def spread_y(k, arriving):
        row = wrap(y - k, NY) if arriving else y
        block = summary.at[pl.ds(2 * row, 2)]
        return remote(block, block, hs.at[k - 1], hr.at[k - 1], dp, wrap(y + k, NY), z)

    for k in (2, 1, 3):
        spread_y(k, False).start()
    for k in range(1, NY):
        spread_y(k, True).wait_recv()
    keep_own.wait()
    for k in range(1, groups):
        move(k, True).wait_recv()
        move(k, False).wait_send()
    for k in range(1, NY):
        swap_y(k).wait_send()
        spread_y(k, False).wait_send()
    for k in range(1, NZ):
        swap_z(k).wait_send()
        spread_z(k, False).wait_send()


def combine(part, sent):
    heads, lines, points = part.shape
    head_size = lines - 8
    groups = sent.shape[0]
    dma = pltpu.SemaphoreType.DMA
    return pl.pallas_call(
        combine_kernel,
        out_shape=(
            jax.ShapeDtypeStruct((heads, head_size, points), jnp.bfloat16),
            jax.ShapeDtypeStruct(sent.shape, sent.dtype),
        ),
        in_specs=[VMEM, VMEM],
        out_specs=(VMEM, VMEM),
        scratch_shapes=[
            pltpu.VMEM((NY - 1, 2, lines, points), jnp.float32),
            pltpu.VMEM((NZ, head_size // 4 + 8, 128), jnp.float32),
            pltpu.VMEM((NZ - 1, head_size // 4 + 8, 128), jnp.float32),
            pltpu.VMEM((head_size // 4, 128), jnp.bfloat16),
            dma((2,)),
            dma((groups - 1,)), dma((groups - 1,)),
            dma((NY - 1,)), dma((NY - 1,)),
            dma((NZ - 1,)), dma((NZ - 1,)),
            dma((NZ - 1,)), dma((NZ - 1,)),
            dma((NY - 1,)), dma((NY - 1,)),
        ],
        compiler_params=pltpu.CompilerParams(collective_id=1, has_side_effects=True),
        name="combine",
    )(part, sent)


def local(peak_rows, row_route, inducing, w_key, w_value, w_query):
    rows = peak_rows[0]
    row_count, width = rows.shape
    groups = lax.axis_size("dp")
    points = inducing.shape[0]
    kv, qf = gather_weights(w_key, w_value, w_query)
    local_queries, sent, part = attend(rows, row_route[0], inducing, kv, qf, groups)
    summary, moved = combine(part, sent.reshape(groups, 16, width))
    summary = summary.transpose(2, 0, 1).reshape(points, width)
    return summary[None], local_queries[None], moved.reshape(1, groups * 16, width)


def solution(mesh):
    placed = (
        P("dp", "ctx", None),
        P("dp", "ctx"),
        P(),
        P("ctx", None),
        P("ctx", None),
        P("ctx", None),
    )
    return jax.shard_map(
        local,
        mesh=mesh,
        in_specs=placed,
        out_specs=(P("dp", None, None), P("dp", "ctx", None), P("dp", "ctx", None)),
        check_vma=False,
    )
```

```python
import math

import jax
import jax.numpy as jnp
from jax import lax
from jax.experimental import pallas as pl
from jax.experimental.pallas import tpu as pltpu
from jax.sharding import PartitionSpec as P

HEADS = 8
NY = 4
NZ = 16
HALF = NZ // 2
SCORE_FLOOR = -1e30
MESH = pl.DeviceIdType.MESH
VMEM = pl.BlockSpec(memory_space=pltpu.VMEM)

FAR = (1, NZ - 1)
ORDER = (8, 7, 9, 6, 10, 5, 11, 4, 12, 3, 13, 2, 14, 1, 15)


def place():
    dp = lax.axis_index("dp")
    ctx = lax.axis_index("ctx")
    return dp, lax.div(ctx, NZ), lax.rem(ctx, NZ)


def wrap(value, size):
    return lax.rem(value + size, size)


def remote(src, dst, send_sem, recv_sem, dp, y, z):
    return pltpu.make_async_remote_copy(
        src_ref=src,
        dst_ref=dst,
        send_sem=send_sem,
        recv_sem=recv_sem,
        device_id=(dp, y * NZ + z),
        device_id_type=MESH,
    )


def greet(partners):
    barrier = pltpu.get_barrier_semaphore()
    for dp, y, z in partners:
        pl.semaphore_signal(barrier, inc=1, device_id=(dp, y * NZ + z), device_id_type=MESH)
    pl.semaphore_wait(barrier, len(partners))


def kernel(
    rows, route, inducing, wk, wv, wq,
    summary, local_out, moved,
    kv, qf, sent, own_value, own_stat, out_value, out_stat, in_value, in_stat,
    to_value, to_stat, from_value, from_stat, piece,
    local_sem, zas, zar, zqs, zqr, ys, yr, fs, fr, qs, qr, pas, par, pqs, pqr,
    ms, mr, vs, vr, ss, sr, zvs, zvr, zss, zsr, gs, gr, hs, hr,
):
    dp, y, z = place()
    core = lax.rem(dp, 2)
    partner = dp + 1 - 2 * core
    groups = moved.shape[0]
    row_count, width = rows.shape
    points = inducing.shape[0]
    head_size = width // HEADS
    half_width = width // 2
    quarter = head_size // 4
    cols = pl.ds(pl.multiple_of(core * half_width, half_width), half_width)

    def shifted(step, way):
        return wrap(z - step if way == 0 else z + step, NZ)

    def kv_ring(step, way, arriving):
        block = kv.at[core, shifted(step + 1 if arriving else step, way), y]
        target = wrap(z + 1 if way == 0 else z - 1, NZ)
        return remote(block, block, zas.at[way, step], zar.at[way, step], dp, y, target)

    def q_ring(step, way, arriving):
        block = qf.at[core, shifted(step + 1 if arriving else step, way)]
        target = wrap(z + 1 if way == 0 else z - 1, NZ)
        return remote(block, block, zqs.at[way, step], zqr.at[way, step], dp, y, target)

    def kv_side(step, way, side, arriving):
        row = y if not arriving else wrap(y - 1 if side == 0 else y + 1, NY)
        block = kv.at[core, shifted(step, way), row]
        slot = 2 * step + way
        target = wrap(y + 1 if side == 0 else y - 1, NY)
        return remote(block, block, ys.at[side, slot], yr.at[side, slot], dp, target, z)

    def kv_pass(step, way, side, arriving):
        hops = 2 if arriving else 1
        row = wrap(y - hops if side == 0 else y + hops, NY)
        block = kv.at[core, shifted(step, way), row, side]
        slot = 2 * step + way
        target = wrap(y + 1 if side == 0 else y - 1, NY)
        return remote(block, block, fs.at[side, slot], fr.at[side, slot], dp, target, z)

    def kv_swap(step, way, arriving):
        block = kv.at[1 - core if arriving else core, shifted(step, way)]
        slot = 2 * step + way
        return remote(block, block, pas.at[slot], par.at[slot], partner, y, z)

    def q_swap(step, way, arriving):
        block = qf.at[1 - core if arriving else core, shifted(step, way)]
        slot = 2 * step + way
        return remote(block, block, pqs.at[slot], pqr.at[slot], partner, y, z)

    def q_side(hop, arriving):
        row = wrap(y - hop, NY) if arriving else y
        block = qf.at[core, z, row]
        return remote(block, block, qs.at[hop - 1], qr.at[hop - 1], dp, wrap(y + hop, NY), z)

    def stage_kv(step, ways, onward):
        for way in ways:
            if not (isinstance(step, int) and step == 0):
                kv_ring(step - 1, way, True).wait_recv()
        for way in onward:
            kv_ring(step, way, False).start()
        for way in ways:
            for side in (0, 1):
                kv_side(step, way, side, False).start()

    def stage_q(step, ways, onward):
        for way in ways:
            if not (isinstance(step, int) and step == 0):
                q_ring(step - 1, way, True).wait_recv()
        for way in onward:
            q_ring(step, way, False).start()
        for way in ways:
            q_swap(step, way, False).start()

    def stage_pass(step, ways):
        for way in ways:
            for side in (0, 1):
                kv_side(step, way, side, True).wait_recv()
                kv_pass(step, way, side, False).start()

    def stage_swap(step, ways):
        for way in ways:
            for side in (0, 1):
                kv_pass(step, way, side, True).wait_recv()
            kv_swap(step, way, False).start()

    own = [
        pltpu.make_async_copy(wk.at[:, cols], kv.at[core, z, y, 0], local_sem.at[0]),
        pltpu.make_async_copy(wv.at[:, cols], kv.at[core, z, y, 1], local_sem.at[1]),
        pltpu.make_async_copy(wq.at[:, cols], qf.at[core, z, y], local_sem.at[2]),
    ]
    for copy in own:
        copy.start()
    greet(
        [(wrap(dp + k, groups), y, z) for k in range(1, groups)]
        + [(dp, wrap(y + k, NY), z) for k in range(1, NY)]
        + [(dp, y, wrap(z + k, NZ)) for k in FAR]
    )
    for copy in own:
        copy.wait()

    both = (0, 1)
    for hop in (1, 3, 2):
        q_side(hop, False).start()
    stage_kv(0, (0,), both)
    for hop in (1, 3, 2):
        q_side(hop, True).wait_recv()
    stage_q(0, (0,), both)
    stage_kv(1, both, both)
    stage_q(1, both, both)
    stage_pass(0, (0,))

    def body(step, carry):
        stage_kv(step, both, both)
        stage_q(step, both, both)
        stage_pass(step - 1, both)

        @pl.when(step > 2)
        def _():
            stage_swap(step - 2, both)

        @pl.when(step == 2)
        def _():
            stage_swap(0, (0,))

        return carry

    lax.fori_loop(2, HALF - 1, body, 0)
    last = HALF - 1
    stage_kv(last, both, (0,))
    stage_q(last, both, (0,))
    stage_pass(last - 1, both)
    stage_swap(last - 2, both)
    stage_kv(HALF, (0,), ())
    stage_q(HALF, (0,), ())
    stage_pass(last, both)
    stage_swap(last - 1, both)
    stage_pass(HALF, (0,))
    stage_swap(last, both)
    stage_swap(HALF, (0,))


    lane_route = jnp.broadcast_to(route[...], (groups, row_count))
    target = lax.broadcasted_iota(jnp.int32, (groups, row_count), 0)
    outgoing = jnp.where((lane_route == target) & (target != dp), 1.0, 0.0)
    before = lax.broadcasted_iota(jnp.int32, (row_count, row_count), 0)
    after = lax.broadcasted_iota(jnp.int32, (row_count, row_count), 1)
    ramp = jnp.where(before <= after, 1.0, 0.0).astype(jnp.bfloat16)
    rank = jnp.dot(outgoing.astype(jnp.bfloat16), ramp, preferred_element_type=jnp.float32)
    slot = lax.broadcasted_iota(jnp.int32, (16, row_count), 0).astype(jnp.float32) + 1.0
    picks = jnp.concatenate(
        [
            jnp.where(
                (jnp.broadcast_to(rank[g : g + 1], (16, row_count)) == slot)
                & (jnp.broadcast_to(outgoing[g : g + 1], (16, row_count)) > 0.5),
                1.0,
                0.0,
            )
            for g in range(groups)
        ],
        axis=0,
    ).astype(jnp.bfloat16)
    spread_route = jnp.broadcast_to(route[...].astype(jnp.float32), (row_count, row_count))
    column = jnp.sum(jnp.where(before == after, spread_route, 0.0), axis=1, keepdims=True)
    live = column > -0.5
    keep = column == dp.astype(jnp.float32)

    def product(weights):
        total = None
        span = width // NY
        for line in range(NY):
            block = weights(line)
            term = jnp.dot(
                rows[:, line * span : (line + 1) * span],
                block.reshape(span, block.shape[-1]),
                preferred_element_type=jnp.float32,
            )
            total = term if total is None else total + term
        return total.astype(jnp.bfloat16)

    def settle_kv(step, ways):
        for way in ways:
            kv_swap(step, way, True).wait_recv()

    def settle_q(step, ways):
        for way in ways:
            q_swap(step, way, True).wait_recv()

    def settle_kv_body(step, carry):
        settle_kv(step, both)
        return carry

    def settle_q_body(step, carry):
        settle_q(step, both)
        return carry

    settle_kv(0, (0,))
    lax.fori_loop(1, HALF, settle_kv_body, 0)
    settle_kv(HALF, (0,))

    def swap_value(k):
        there = wrap(y + k, NY)
        return remote(
            out_value.at[k - 1], in_value.at[k - 1], vs.at[k - 1], vr.at[k - 1], dp, there, z
        )

    def swap_stat(k):
        there = wrap(y + k, NY)
        return remote(
            out_stat.at[k - 1], in_stat.at[k - 1], ss.at[k - 1], sr.at[k - 1], dp, there, z
        )

    stat_row = lax.broadcasted_iota(jnp.int32, (8, points), 0)
    scale = jnp.float32(1.0 / math.sqrt(head_size))
    pair = 2 * head_size
    for k in (2, 1, 3, 0):
        block = wrap(y + k, NY)
        side = lax.div(block, 2)
        lanes = pl.ds(pl.multiple_of(lax.rem(block, 2) * pair, pair), pair)
        keys = product(lambda line: kv[side, :, line, 0, :, lanes])
        values = product(lambda line: kv[side, :, line, 1, :, lanes])
        for sub in range(2):
            span = slice(sub * head_size, (sub + 1) * head_size)
            offset = pl.multiple_of(block * pair + sub * head_size, head_size)
            scores = lax.dot_general(
                keys[:, span],
                inducing[:, pl.ds(offset, head_size)],
                (((1,), (1,)), ((), ())),
                preferred_element_type=jnp.float32,
            )
            scores = jnp.where(live, scores * scale, jnp.float32(SCORE_FLOOR))
            top = jnp.max(scores, axis=0, keepdims=True)
            terms = jnp.where(live, jnp.exp(scores - top), 0.0)
            total = jnp.sum(terms, axis=0, keepdims=True)
            weighted = lax.dot_general(
                values[:, span],
                terms.astype(jnp.bfloat16),
                (((0,), (0,)), ((), ())),
                preferred_element_type=jnp.float32,
            )
            stats = jnp.where(
                stat_row < 4,
                jnp.broadcast_to(top, (8, points)),
                jnp.broadcast_to(total, (8, points)),
            )
            if k == 0:
                own_value[sub] = weighted
                own_stat[sub] = stats
            else:
                out_value[k - 1, sub] = weighted.astype(jnp.bfloat16)
                out_stat[k - 1, sub] = stats
        if k:
            swap_stat(k).start()
            swap_value(k).start()

    settle_q(0, (0,))
    lax.fori_loop(1, HALF, settle_q_body, 0)
    settle_q(HALF, (0,))
    for block in range(NY):
        lanes = slice((block % 2) * pair, (block % 2 + 1) * pair)
        queries = product(lambda line: qf[block // 2, :, line, :, lanes])
        span = slice(block * pair, (block + 1) * pair)
        local_out[:, span] = jnp.where(keep, queries.astype(jnp.float32), 0.0).astype(jnp.bfloat16)
        chosen = jnp.dot(picks, queries, preferred_element_type=jnp.float32)
        sent[:, :, span] = chosen.astype(jnp.bfloat16).reshape(groups, 16, pair)

    def move(k, arriving):
        there = wrap(dp + k, groups)
        place_at = wrap(dp - k, groups) if arriving else dp
        return remote(sent.at[there], moved.at[place_at], ms.at[k - 1], mr.at[k - 1], there, y, z)

    for k in range(1, groups):
        move(k, False).start()
    keep_own = pltpu.make_async_copy(sent.at[dp], moved.at[dp], local_sem.at[3])
    keep_own.start()

    for k in (2, 1, 3):
        swap_stat(k).wait_recv()
        swap_value(k).wait_recv()

    stat_row = lax.broadcasted_iota(jnp.int32, (8, 128), 0)
    for head in range(2):
        for half in range(2):
            lanes = slice(half * 128, half * 128 + 128)
            values = [own_value.at[head]] + [in_value.at[k, head] for k in range(NY - 1)]
            stats = [own_stat.at[head]] + [in_stat.at[k, head] for k in range(NY - 1)]
            tops = [s[0:1, lanes] for s in stats]
            totals = [s[4:5, lanes] for s in stats]
            top = tops[0]
            for other in tops[1:]:
                top = jnp.maximum(top, other)
            shares = [jnp.exp(t - top) for t in tops]
            total = totals[0] * shares[0]
            for other, share in zip(totals[1:], shares[1:]):
                total = total + other * share
            to_stat[2 * head + half] = jnp.where(
                stat_row < 4, jnp.broadcast_to(top, (8, 128)), jnp.broadcast_to(total, (8, 128))
            )
            for group in range(4):
                lines = slice(group * quarter, (group + 1) * quarter)
                value = values[0][lines, lanes] * shares[0]
                for source, share in zip(values[1:], shares[1:]):
                    value = value + source[lines, lanes].astype(jnp.float32) * share
                to_value[head * 8 + half * 4 + group] = value.astype(jnp.bfloat16)

    def part_stat(k):
        there = wrap(z + k, NZ)
        return remote(
            to_stat.at[lax.div(there, 4)], from_stat.at[k - 1], zss.at[k - 1], zsr.at[k - 1],
            dp, y, there,
        )

    def part_value(k):
        there = wrap(z + k, NZ)
        return remote(
            to_value.at[there], from_value.at[k - 1], zvs.at[k - 1], zvr.at[k - 1], dp, y, there
        )

    for k in ORDER:
        part_stat(k).start()
        part_value(k).start()
    for k in reversed(ORDER):
        part_stat(k).wait_recv()
        part_value(k).wait_recv()

    values = [to_value.at[z]] + [from_value.at[k] for k in range(NZ - 1)]
    stats = [to_stat.at[lax.div(z, 4)]] + [from_stat.at[k] for k in range(NZ - 1)]
    tops = [s[0:1, :] for s in stats]
    top = tops[0]
    for other in tops[1:]:
        top = jnp.maximum(top, other)
    value = None
    total = None
    for source, stat, own_top in zip(values, stats, tops):
        share = jnp.exp(own_top - top)
        term = source[...].astype(jnp.float32) * share
        count = stat[4:5, :] * share
        value = term if value is None else value + term
        total = count if total is None else total + count
    piece[...] = (value / total).astype(jnp.bfloat16)

    def spot(row, there):
        return summary.at[
            2 * row + lax.div(there, 8),
            pl.ds(pl.multiple_of(lax.rem(there, 4) * quarter, quarter), quarter),
            pl.ds(pl.multiple_of(lax.rem(lax.div(there, 4), 2) * 128, 128), 128),
        ]

    def spread_z(k, arriving):
        owner = wrap(z - k, NZ) if arriving else z
        return remote(
            piece, spot(y, owner), gs.at[k - 1], gr.at[k - 1], dp, y, wrap(z + k, NZ)
        )

    def spread_y(k, j, arriving):
        block = spot(wrap(y - j, NY) if arriving else y, wrap(z - k, NZ))
        source = piece if k == 0 else block
        return remote(
            source, block, hs.at[j - 1, k], hr.at[j - 1, k], dp, wrap(y + j, NY), z
        )

    for k in ORDER:
        spread_z(k, False).start()
    own_piece = pltpu.make_async_copy(piece, spot(y, z), local_sem.at[4])
    own_piece.start()
    for j in (2, 1, 3):
        spread_y(0, j, False).start()
    for k in reversed(ORDER):
        spread_z(k, True).wait_recv()
        for j in (2, 1, 3):
            spread_y(k, j, False).start()
    own_piece.wait()
    keep_own.wait()
    for k in range(NZ):
        for j in range(1, NY):
            spread_y(k, j, True).wait_recv()
    for k in range(1, groups):
        move(k, True).wait_recv()
        move(k, False).wait_send()
    for k in range(1, NY):
        swap_value(k).wait_send()
        swap_stat(k).wait_send()
    for k in range(1, NZ):
        part_value(k).wait_send()
        part_stat(k).wait_send()
        spread_z(k, False).wait_send()
    for k in range(NZ):
        for j in range(1, NY):
            spread_y(k, j, False).wait_send()

    for hop in (1, 2, 3):
        q_side(hop, False).wait_send()

    def finish_slot(step, ways):
        for way in ways:
            kv_swap(step, way, False).wait_send()
            q_swap(step, way, False).wait_send()
            for side in (0, 1):
                kv_side(step, way, side, False).wait_send()
                kv_pass(step, way, side, False).wait_send()

    def finish_ring(step, ways):
        for way in ways:
            kv_ring(step, way, False).wait_send()
            q_ring(step, way, False).wait_send()

    finish_slot(0, (0,))
    finish_ring(0, both)

    def finish(step, carry):
        finish_slot(step, both)
        finish_ring(step, both)
        return carry

    lax.fori_loop(1, last, finish, 0)
    finish_slot(last, both)
    finish_ring(last, (0,))
    finish_slot(HALF, (0,))


def local(peak_rows, row_route, inducing, w_key, w_value, w_query):
    rows = peak_rows[0]
    row_count, width = rows.shape
    depth = w_key.shape[0]
    groups = lax.axis_size("dp")
    points = inducing.shape[0]
    head_size = width // HEADS
    half = width // 2
    quarter = head_size // 4
    slots = 2 * HALF + 1
    dma = pltpu.SemaphoreType.DMA
    low, wide = jnp.bfloat16, jnp.float32
    summary, local_queries, moved = pl.pallas_call(
        kernel,
        out_shape=(
            jax.ShapeDtypeStruct((HEADS, head_size, points), low),
            jax.ShapeDtypeStruct((row_count, width), low),
            jax.ShapeDtypeStruct((groups, 16, width), low),
        ),
        in_specs=[VMEM] * 6,
        out_specs=(VMEM,) * 3,
        scratch_shapes=[
            pltpu.VMEM((2, NZ, NY, 2, depth, half), low),
            pltpu.VMEM((2, NZ, NY, depth, half), low),
            pltpu.VMEM((groups, 16, width), low),
            pltpu.VMEM((2, head_size, points), wide),
            pltpu.VMEM((2, 8, points), wide),
            pltpu.VMEM((NY - 1, 2, head_size, points), low),
            pltpu.VMEM((NY - 1, 2, 8, points), wide),
            pltpu.VMEM((NY - 1, 2, head_size, points), low),
            pltpu.VMEM((NY - 1, 2, 8, points), wide),
            pltpu.VMEM((NZ, quarter, 128), low),
            pltpu.VMEM((4, 8, 128), wide),
            pltpu.VMEM((NZ - 1, quarter, 128), low),
            pltpu.VMEM((NZ - 1, 8, 128), wide),
            pltpu.VMEM((quarter, 128), low),
            dma((5,)),
            dma((2, HALF)), dma((2, HALF)),
            dma((2, HALF)), dma((2, HALF)),
            dma((2, slots)), dma((2, slots)),
            dma((2, slots)), dma((2, slots)),
            dma((NY - 1,)), dma((NY - 1,)),
            dma((slots,)), dma((slots,)),
            dma((slots,)), dma((slots,)),
            dma((groups - 1,)), dma((groups - 1,)),
            dma((NY - 1,)), dma((NY - 1,)),
            dma((NY - 1,)), dma((NY - 1,)),
            dma((NZ - 1,)), dma((NZ - 1,)),
            dma((NZ - 1,)), dma((NZ - 1,)),
            dma((NZ - 1,)), dma((NZ - 1,)),
            dma((NY - 1, NZ)), dma((NY - 1, NZ)),
        ],
        compiler_params=pltpu.CompilerParams(collective_id=0, has_side_effects=True),
        name="encode",
    )(rows, row_route, inducing, w_key, w_value, w_query)
    summary = summary.transpose(2, 0, 1).reshape(points, width)
    return summary[None], local_queries[None], moved.reshape(1, groups * 16, width)


def solution(mesh):
    placed = (
        P("dp", "ctx", None),
        P("dp", "ctx"),
        P(),
        P("ctx", None),
        P("ctx", None),
        P("ctx", None),
    )
    return jax.shard_map(
        local,
        mesh=mesh,
        in_specs=placed,
        out_specs=(P("dp", None, None), P("dp", "ctx", None), P("dp", "ctx", None)),
        check_vma=False,
    )
```

```python
import math

import jax
import jax.numpy as jnp
from jax import lax
from jax.experimental import pallas as pl
from jax.experimental.pallas import tpu as pltpu
from jax.sharding import PartitionSpec as P

HEADS = 8
NY = 4
NZ = 16
SCORE_FLOOR = -1e30
MESH = pl.DeviceIdType.MESH
VMEM = pl.BlockSpec(memory_space=pltpu.VMEM)

NX = 4
HOPS = (
    (0, 4, None), (0, -4, None),
    (-4, 4, 0), (4, -4, 1),
    (0, 1, None), (0, -1, None), (0, 2, None), (0, -2, None),
    (-4, 1, None), (-4, -1, None), (-4, 2, None),
    (4, 1, None), (4, -1, None), (4, -2, None),
    (8, 1, None), (8, -1, None),
)
BLOCKS = (0, -1, 1, -4, 4, -2, 2, 8, -5, 3, -3, 5, -6, 6, 7, -7)
FAR = (1, 2, 4, NZ - 4, NZ - 2, NZ - 1)
ORDER = (8, 7, 9, 6, 10, 5, 11, 4, 12, 3, 13, 2, 14, 1, 15)


def place():
    dp = lax.axis_index("dp")
    ctx = lax.axis_index("ctx")
    return dp, lax.div(ctx, NZ), lax.rem(ctx, NZ)


def wrap(value, size):
    return lax.rem(value + size, size)


def remote(src, dst, send_sem, recv_sem, dp, y, z):
    return pltpu.make_async_remote_copy(
        src_ref=src,
        dst_ref=dst,
        send_sem=send_sem,
        recv_sem=recv_sem,
        device_id=(dp, y * NZ + z),
        device_id_type=MESH,
    )


def greet(partners):
    barrier = pltpu.get_barrier_semaphore()
    for dp, y, z in partners:
        pl.semaphore_signal(barrier, inc=1, device_id=(dp, y * NZ + z), device_id_type=MESH)
    pl.semaphore_wait(barrier, len(partners))


def kernel(
    rows, route, inducing, wk, wv, wq,
    summary, local_out, moved,
    kv, qf, sent, own_value, own_stat, out_value, out_stat, in_value, in_stat,
    to_value, to_stat, from_value, from_stat, piece,
    local_sem, zas, zar, zqs, zqr, ys, yr, fs, fr, pas, par, qys, qyr, qxs, qxr, qfs, qfr, pqs, pqr,
    ms, mr, vs, vr, ss, sr, zvs, zvr, zss, zsr, gs, gr, hs, hr,
):
    dp, y, z = place()
    core = lax.rem(dp, 2)
    partner = dp + 1 - 2 * core
    groups = moved.shape[0]
    row_count, width = rows.shape
    points = inducing.shape[0]
    head_size = width // HEADS
    half_width = width // 2
    quarter = head_size // 4
    cols = pl.ds(pl.multiple_of(core * half_width, half_width), half_width)

    column_x = lax.div(dp, 2)
    eighth = width // (2 * NX)
    q_cols = pl.ds(pl.multiple_of(core * half_width + column_x * eighth, eighth), eighth)

    def at_z(offset):
        return wrap(z + offset, NZ)

    def kv_hop(hop, arriving):
        block, ahead, part = HOPS[hop]
        spot = kv.at[core, at_z(block - ahead if arriving else block), y]
        if part is not None:
            spot = spot.at[part]
        return remote(spot, spot, zas.at[hop], zar.at[hop], dp, y, at_z(ahead))

    def q_hop(hop, arriving):
        block, ahead, _ = HOPS[hop]
        spot = qf.at[core, column_x, y, at_z(block - ahead if arriving else block)]
        return remote(spot, spot, zqs.at[hop], zqr.at[hop], dp, y, at_z(ahead))

    def kv_side(block, side, arriving):
        row = y if not arriving else wrap(y - 1 if side == 0 else y + 1, NY)
        spot = kv.at[core, at_z(block), row]
        slot = BLOCKS.index(block)
        target = wrap(y + 1 if side == 0 else y - 1, NY)
        return remote(spot, spot, ys.at[side, slot], yr.at[side, slot], dp, target, z)

    def kv_pass(block, side, arriving):
        hops = 2 if arriving else 1
        row = wrap(y - hops if side == 0 else y + hops, NY)
        spot = kv.at[core, at_z(block), row, side]
        slot = BLOCKS.index(block)
        target = wrap(y + 1 if side == 0 else y - 1, NY)
        return remote(spot, spot, fs.at[side, slot], fr.at[side, slot], dp, target, z)

    def kv_swap(block, arriving):
        spot = kv.at[1 - core if arriving else core, at_z(block)]
        slot = BLOCKS.index(block)
        return remote(spot, spot, pas.at[slot], par.at[slot], partner, y, z)

    def q_side(k, arriving):
        spot = qf.at[core, column_x, wrap(y - k, NY) if arriving else y]
        return remote(spot, spot, qys.at[k - 1], qyr.at[k - 1], dp, wrap(y + k, NY), z)

    def q_cross(k, side, arriving):
        step = 1 if side == 0 else -1
        source = wrap(column_x - step, NX) if arriving else column_x
        spot = qf.at[core, source, wrap(y - k, NY)]
        target = 2 * wrap(column_x + step, NX) + core
        return remote(spot, spot, qxs.at[side, k], qxr.at[side, k], target, y, z)

    def q_pass(k, arriving):
        step = 1 if k < 2 else -1
        source = wrap(column_x - (2 * step if arriving else step), NX)
        spot = qf.at[core, source, wrap(y - k, NY)]
        target = 2 * wrap(column_x + step, NX) + core
        return remote(spot, spot, qfs.at[k], qfr.at[k], target, y, z)

    def q_swap(k, arriving):
        spot = qf.at[1 - core if arriving else core, wrap(column_x + k, NX)]
        return remote(spot, spot, pqs.at[k], pqr.at[k], partner, y, z)

    own = [
        pltpu.make_async_copy(wk.at[:, cols], kv.at[core, z, y, 0], local_sem.at[0]),
        pltpu.make_async_copy(wv.at[:, cols], kv.at[core, z, y, 1], local_sem.at[1]),
        pltpu.make_async_copy(wq.at[:, q_cols], qf.at[core, column_x, y, z], local_sem.at[2]),
    ]
    for copy in own:
        copy.start()
    greet(
        [(wrap(dp + k, groups), y, z) for k in range(1, groups)]
        + [(dp, wrap(y + k, NY), z) for k in range(1, NY)]
        + [(dp, y, wrap(z + k, NZ)) for k in FAR]
    )
    for copy in own:
        copy.wait()

    def side_out(*blocks):
        for block in blocks:
            for side in (0, 1):
                kv_side(block, side, False).start()

    def pass_on(*blocks):
        for block in blocks:
            for side in (0, 1):
                kv_side(block, side, True).wait_recv()
                kv_pass(block, side, False).start()

    def swap_out(*blocks):
        for block in blocks:
            for side in (0, 1):
                kv_pass(block, side, True).wait_recv()
            kv_swap(block, False).start()

    def go(*hops):
        for hop in hops:
            kv_hop(hop, False).start()

    def arrive(*hops):
        for hop in hops:
            kv_hop(hop, True).wait_recv()

    q_hops = tuple(hop for hop in range(len(HOPS)) if hop != 3)

    def q_go(*hops):
        for hop in hops:
            q_hop(hop, False).start()

    def q_arrive(*hops):
        for hop in hops:
            q_hop(hop, True).wait_recv()

    go(0, 1, 4, 5, 6, 7)
    side_out(0)
    q_go(0, 1, 4, 5, 6, 7)
    arrive(4, 5)
    side_out(-1, 1)
    arrive(0)
    go(2, 8, 9, 10)
    arrive(1)
    go(3, 11, 12, 13)
    side_out(-4, 4)
    q_arrive(0, 1)
    q_go(2, 8, 9, 10, 11, 12, 13)
    pass_on(0)
    arrive(6, 7)
    side_out(-2, 2)
    pass_on(-1, 1)
    arrive(2, 3)
    go(14, 15)
    side_out(8)
    q_arrive(2)
    q_go(14, 15)
    arrive(8, 9, 11, 12)
    side_out(-5, 3, -3, 5)
    arrive(10, 13)
    side_out(-6, 6)
    arrive(14, 15)
    side_out(7, -7)
    pass_on(-4, 4)
    swap_out(0)
    q_arrive(*(hop for hop in q_hops if hop not in (0, 1, 2)))
    for k in (2, 1, 3):
        q_side(k, False).start()
    for side in (0, 1):
        q_cross(0, side, False).start()
    pass_on(-2, 2)
    swap_out(-1, 1)
    pass_on(8, -5)
    swap_out(-4, 4)
    pass_on(3, -3)
    swap_out(-2, 2)
    pass_on(5, -6)
    swap_out(8, -5)
    for k in (1, 3, 2):
        q_side(k, True).wait_recv()
        for side in (0, 1):
            q_cross(k, side, False).start()
    pass_on(6, 7, -7)
    swap_out(3, -3, 5, -6)
    for k in range(NY):
        for side in (0, 1):
            q_cross(k, side, True).wait_recv()
    for k in range(NY):
        q_pass(k, False).start()
    for k in (0, 1, 3):
        q_swap(k, False).start()
    swap_out(6, 7, -7)

    lane_route = jnp.broadcast_to(route[...], (groups, row_count))
    target = lax.broadcasted_iota(jnp.int32, (groups, row_count), 0)
    outgoing = jnp.where((lane_route == target) & (target != dp), 1.0, 0.0)
    before = lax.broadcasted_iota(jnp.int32, (row_count, row_count), 0)
    after = lax.broadcasted_iota(jnp.int32, (row_count, row_count), 1)
    ramp = jnp.where(before <= after, 1.0, 0.0).astype(jnp.bfloat16)
    rank = jnp.dot(outgoing.astype(jnp.bfloat16), ramp, preferred_element_type=jnp.float32)
    slot = lax.broadcasted_iota(jnp.int32, (16, row_count), 0).astype(jnp.float32) + 1.0
    picks = jnp.concatenate(
        [
            jnp.where(
                (jnp.broadcast_to(rank[g : g + 1], (16, row_count)) == slot)
                & (jnp.broadcast_to(outgoing[g : g + 1], (16, row_count)) > 0.5),
                1.0,
                0.0,
            )
            for g in range(groups)
        ],
        axis=0,
    ).astype(jnp.bfloat16)
    spread_route = jnp.broadcast_to(route[...].astype(jnp.float32), (row_count, row_count))
    column = jnp.sum(jnp.where(before == after, spread_route, 0.0), axis=1, keepdims=True)
    live = column > -0.5
    keep = column == dp.astype(jnp.float32)

    def product(weights):
        total = None
        span = width // NY
        for line in range(NY):
            block = weights(line)
            term = jnp.dot(
                rows[:, line * span : (line + 1) * span],
                block.reshape(span, block.shape[-1]),
                preferred_element_type=jnp.float32,
            )
            total = term if total is None else total + term
        return total.astype(jnp.bfloat16)

    for block in BLOCKS:
        kv_swap(block, True).wait_recv()

    def swap_value(k):
        there = wrap(y + k, NY)
        return remote(
            out_value.at[k - 1], in_value.at[k - 1], vs.at[k - 1], vr.at[k - 1], dp, there, z
        )

    def swap_stat(k):
        there = wrap(y + k, NY)
        return remote(
            out_stat.at[k - 1], in_stat.at[k - 1], ss.at[k - 1], sr.at[k - 1], dp, there, z
        )

    stat_row = lax.broadcasted_iota(jnp.int32, (8, points), 0)
    scale = jnp.float32(1.0 / math.sqrt(head_size))
    pair = 2 * head_size
    for k in (2, 1, 3, 0):
        block = wrap(y + k, NY)
        side = lax.div(block, 2)
        lanes = pl.ds(pl.multiple_of(lax.rem(block, 2) * pair, pair), pair)
        keys = product(lambda line: kv[side, :, line, 0, :, lanes])
        values = product(lambda line: kv[side, :, line, 1, :, lanes])
        for sub in range(2):
            span = slice(sub * head_size, (sub + 1) * head_size)
            offset = pl.multiple_of(block * pair + sub * head_size, head_size)
            scores = lax.dot_general(
                keys[:, span],
                inducing[:, pl.ds(offset, head_size)],
                (((1,), (1,)), ((), ())),
                preferred_element_type=jnp.float32,
            )
            scores = jnp.where(live, scores * scale, jnp.float32(SCORE_FLOOR))
            top = jnp.max(scores, axis=0, keepdims=True)
            terms = jnp.where(live, jnp.exp(scores - top), 0.0)
            total = jnp.sum(terms, axis=0, keepdims=True)
            weighted = lax.dot_general(
                values[:, span],
                terms.astype(jnp.bfloat16),
                (((0,), (0,)), ((), ())),
                preferred_element_type=jnp.float32,
            )
            stats = jnp.where(
                stat_row < 4,
                jnp.broadcast_to(top, (8, points)),
                jnp.broadcast_to(total, (8, points)),
            )
            if k == 0:
                own_value[sub] = weighted
                own_stat[sub] = stats
            else:
                out_value[k - 1, sub] = weighted.astype(jnp.bfloat16)
                out_stat[k - 1, sub] = stats
        if k:
            swap_stat(k).start()
            swap_value(k).start()

    for k in range(NY):
        q_pass(k, True).wait_recv()
    q_swap(2, False).start()
    for k in range(NX):
        q_swap(k, True).wait_recv()
    for block in range(NY):
        first = 2 * (block % 2)
        queries = product(
            lambda line: jnp.concatenate(
                [
                    qf[block // 2, first + e, line].reshape(width // NY, eighth)
                    for e in range(2)
                ],
                axis=1,
            )
        )
        span = slice(block * pair, (block + 1) * pair)
        local_out[:, span] = jnp.where(keep, queries.astype(jnp.float32), 0.0).astype(jnp.bfloat16)
        chosen = jnp.dot(picks, queries, preferred_element_type=jnp.float32)
        sent[:, :, span] = chosen.astype(jnp.bfloat16).reshape(groups, 16, pair)

    def move(k, arriving):
        there = wrap(dp + k, groups)
        place_at = wrap(dp - k, groups) if arriving else dp
        return remote(sent.at[there], moved.at[place_at], ms.at[k - 1], mr.at[k - 1], there, y, z)

    for k in range(1, groups):
        move(k, False).start()
    keep_own = pltpu.make_async_copy(sent.at[dp], moved.at[dp], local_sem.at[3])
    keep_own.start()

    for k in (2, 1, 3):
        swap_stat(k).wait_recv()
        swap_value(k).wait_recv()

    stat_row = lax.broadcasted_iota(jnp.int32, (8, 128), 0)
    for head in range(2):
        for half in range(2):
            lanes = slice(half * 128, half * 128 + 128)
            values = [own_value.at[head]] + [in_value.at[k, head] for k in range(NY - 1)]
            stats = [own_stat.at[head]] + [in_stat.at[k, head] for k in range(NY - 1)]
            tops = [s[0:1, lanes] for s in stats]
            totals = [s[4:5, lanes] for s in stats]
            top = tops[0]
            for other in tops[1:]:
                top = jnp.maximum(top, other)
            shares = [jnp.exp(t - top) for t in tops]
            total = totals[0] * shares[0]
            for other, share in zip(totals[1:], shares[1:]):
                total = total + other * share
            to_stat[2 * head + half] = jnp.where(
                stat_row < 4, jnp.broadcast_to(top, (8, 128)), jnp.broadcast_to(total, (8, 128))
            )
            for group in range(4):
                lines = slice(group * quarter, (group + 1) * quarter)
                value = values[0][lines, lanes] * shares[0]
                for source, share in zip(values[1:], shares[1:]):
                    value = value + source[lines, lanes].astype(jnp.float32) * share
                to_value[head * 8 + half * 4 + group] = value.astype(jnp.bfloat16)

    def part_stat(k):
        there = wrap(z + k, NZ)
        return remote(
            to_stat.at[lax.div(there, 4)], from_stat.at[k - 1], zss.at[k - 1], zsr.at[k - 1],
            dp, y, there,
        )

    def part_value(k):
        there = wrap(z + k, NZ)
        return remote(
            to_value.at[there], from_value.at[k - 1], zvs.at[k - 1], zvr.at[k - 1], dp, y, there
        )

    for k in ORDER:
        part_stat(k).start()
        part_value(k).start()
    for k in reversed(ORDER):
        part_stat(k).wait_recv()
        part_value(k).wait_recv()

    values = [to_value.at[z]] + [from_value.at[k] for k in range(NZ - 1)]
    stats = [to_stat.at[lax.div(z, 4)]] + [from_stat.at[k] for k in range(NZ - 1)]
    tops = [s[0:1, :] for s in stats]
    top = tops[0]
    for other in tops[1:]:
        top = jnp.maximum(top, other)
    value = None
    total = None
    for source, stat, own_top in zip(values, stats, tops):
        share = jnp.exp(own_top - top)
        term = source[...].astype(jnp.float32) * share
        count = stat[4:5, :] * share
        value = term if value is None else value + term
        total = count if total is None else total + count
    piece[...] = (value / total).astype(jnp.bfloat16)

    def spot(row, there):
        return summary.at[
            2 * row + lax.div(there, 8),
            pl.ds(pl.multiple_of(lax.rem(there, 4) * quarter, quarter), quarter),
            pl.ds(pl.multiple_of(lax.rem(lax.div(there, 4), 2) * 128, 128), 128),
        ]

    def spread_z(k, arriving):
        owner = wrap(z - k, NZ) if arriving else z
        return remote(
            piece, spot(y, owner), gs.at[k - 1], gr.at[k - 1], dp, y, wrap(z + k, NZ)
        )

    def spread_y(k, j, arriving):
        block = spot(wrap(y - j, NY) if arriving else y, wrap(z - k, NZ))
        source = piece if k == 0 else block
        return remote(
            source, block, hs.at[j - 1, k], hr.at[j - 1, k], dp, wrap(y + j, NY), z
        )

    for k in ORDER:
        spread_z(k, False).start()
    own_piece = pltpu.make_async_copy(piece, spot(y, z), local_sem.at[4])
    own_piece.start()
    for j in (2, 1, 3):
        spread_y(0, j, False).start()
    for k in reversed(ORDER):
        spread_z(k, True).wait_recv()
        for j in (2, 1, 3):
            spread_y(k, j, False).start()
    own_piece.wait()
    keep_own.wait()
    for k in range(NZ):
        for j in range(1, NY):
            spread_y(k, j, True).wait_recv()
    for k in range(1, groups):
        move(k, True).wait_recv()
        move(k, False).wait_send()
    for k in range(1, NY):
        swap_value(k).wait_send()
        swap_stat(k).wait_send()
    for k in range(1, NZ):
        part_value(k).wait_send()
        part_stat(k).wait_send()
        spread_z(k, False).wait_send()
    for k in range(NZ):
        for j in range(1, NY):
            spread_y(k, j, False).wait_send()

    for hop in range(len(HOPS)):
        kv_hop(hop, False).wait_send()
    for hop in q_hops:
        q_hop(hop, False).wait_send()
    for block in BLOCKS:
        for side in (0, 1):
            kv_side(block, side, False).wait_send()
            kv_pass(block, side, False).wait_send()
        kv_swap(block, False).wait_send()
    for k in range(1, NY):
        q_side(k, False).wait_send()
    for k in range(NY):
        q_pass(k, False).wait_send()
        q_swap(k, False).wait_send()
        for side in (0, 1):
            q_cross(k, side, False).wait_send()


def local(peak_rows, row_route, inducing, w_key, w_value, w_query):
    rows = peak_rows[0]
    row_count, width = rows.shape
    depth = w_key.shape[0]
    groups = lax.axis_size("dp")
    points = inducing.shape[0]
    head_size = width // HEADS
    half = width // 2
    quarter = head_size // 4
    dma = pltpu.SemaphoreType.DMA
    low, wide = jnp.bfloat16, jnp.float32
    summary, local_queries, moved = pl.pallas_call(
        kernel,
        out_shape=(
            jax.ShapeDtypeStruct((HEADS, head_size, points), low),
            jax.ShapeDtypeStruct((row_count, width), low),
            jax.ShapeDtypeStruct((groups, 16, width), low),
        ),
        in_specs=[VMEM] * 6,
        out_specs=(VMEM,) * 3,
        scratch_shapes=[
            pltpu.VMEM((2, NZ, NY, 2, depth, half), low),
            pltpu.VMEM((2, NX, NY, NZ, depth, half // NX), low),
            pltpu.VMEM((groups, 16, width), low),
            pltpu.VMEM((2, head_size, points), wide),
            pltpu.VMEM((2, 8, points), wide),
            pltpu.VMEM((NY - 1, 2, head_size, points), low),
            pltpu.VMEM((NY - 1, 2, 8, points), wide),
            pltpu.VMEM((NY - 1, 2, head_size, points), low),
            pltpu.VMEM((NY - 1, 2, 8, points), wide),
            pltpu.VMEM((NZ, quarter, 128), low),
            pltpu.VMEM((4, 8, 128), wide),
            pltpu.VMEM((NZ - 1, quarter, 128), low),
            pltpu.VMEM((NZ - 1, 8, 128), wide),
            pltpu.VMEM((quarter, 128), low),
            dma((5,)),
            dma((len(HOPS),)), dma((len(HOPS),)),
            dma((len(HOPS),)), dma((len(HOPS),)),
            dma((2, NZ)), dma((2, NZ)),
            dma((2, NZ)), dma((2, NZ)),
            dma((NZ,)), dma((NZ,)),
            dma((NY - 1,)), dma((NY - 1,)),
            dma((2, NY)), dma((2, NY)),
            dma((NY,)), dma((NY,)),
            dma((NX,)), dma((NX,)),
            dma((groups - 1,)), dma((groups - 1,)),
            dma((NY - 1,)), dma((NY - 1,)),
            dma((NY - 1,)), dma((NY - 1,)),
            dma((NZ - 1,)), dma((NZ - 1,)),
            dma((NZ - 1,)), dma((NZ - 1,)),
            dma((NZ - 1,)), dma((NZ - 1,)),
            dma((NY - 1, NZ)), dma((NY - 1, NZ)),
        ],
        compiler_params=pltpu.CompilerParams(collective_id=0, has_side_effects=True),
        name="encode",
    )(rows, row_route, inducing, w_key, w_value, w_query)
    summary = summary.transpose(2, 0, 1).reshape(points, width)
    return summary[None], local_queries[None], moved.reshape(1, groups * 16, width)


def solution(mesh):
    placed = (
        P("dp", "ctx", None),
        P("dp", "ctx"),
        P(),
        P("ctx", None),
        P("ctx", None),
        P("ctx", None),
    )
    return jax.shard_map(
        local,
        mesh=mesh,
        in_specs=placed,
        out_specs=(P("dp", None, None), P("dp", "ctx", None), P("dp", "ctx", None)),
        check_vma=False,
    )
```

```python
import math

import jax
import jax.numpy as jnp
from jax import lax
from jax.experimental import pallas as pl
from jax.experimental.pallas import tpu as pltpu
from jax.sharding import PartitionSpec as P

HEADS = 8
NY = 4
NZ = 16
SCORE_FLOOR = -1e30
MESH = pl.DeviceIdType.MESH
VMEM = pl.BlockSpec(memory_space=pltpu.VMEM)

NX = 4
HOPS = (
    (0, 4, None), (0, -4, None),
    (-4, 4, 0), (4, -4, 1),
    (0, 1, None), (0, -1, None), (0, 2, None), (0, -2, None),
    (-4, 1, None), (-4, -1, None), (-4, 2, None),
    (4, 1, None), (4, -1, None), (4, -2, None),
    (8, 1, None), (8, -1, None),
)
BLOCKS = (0, -1, 1, -4, 4, -2, 2, 8, -5, 3, -3, 5, -6, 6, 7, -7)
FAR = (1, 2, 4, NZ - 4, NZ - 2, NZ - 1)
ORDER = (8, 7, 9, 6, 10, 5, 11, 4, 12, 3, 13, 2, 14, 1, 15)


def place():
    dp = lax.axis_index("dp")
    ctx = lax.axis_index("ctx")
    return dp, lax.div(ctx, NZ), lax.rem(ctx, NZ)


def wrap(value, size):
    return lax.rem(value + size, size)


def remote(src, dst, send_sem, recv_sem, dp, y, z):
    return pltpu.make_async_remote_copy(
        src_ref=src,
        dst_ref=dst,
        send_sem=send_sem,
        recv_sem=recv_sem,
        device_id=(dp, y * NZ + z),
        device_id_type=MESH,
    )


def greet(partners):
    barrier = pltpu.get_barrier_semaphore()
    for dp, y, z in partners:
        pl.semaphore_signal(barrier, inc=1, device_id=(dp, y * NZ + z), device_id_type=MESH)
    pl.semaphore_wait(barrier, len(partners))


def kernel(
    rows, route, inducing, wk, wv, wq,
    summary, local_out, moved,
    kv, qf, sent, out_value, out_stat, in_value, in_stat,
    to_value, to_stat, from_value, from_stat, piece,
    local_sem, zas, zar, zqs, zqr, ys, yr, fs, fr, pas, par, qys, qyr, qxs, qxr, qfs, qfr, pqs, pqr,
    ms, mr, vs, vr, ss, sr, zvs, zvr, zss, zsr, gs, gr, hs, hr,
):
    dp, y, z = place()
    core = lax.rem(dp, 2)
    partner = dp + 1 - 2 * core
    groups = moved.shape[0]
    row_count, width = rows.shape
    points = inducing.shape[0]
    head_size = width // HEADS
    half_width = width // 2
    quarter = head_size // 4
    cols = pl.ds(pl.multiple_of(core * half_width, half_width), half_width)

    column_x = lax.div(dp, 2)
    eighth = width // (2 * NX)
    q_cols = pl.ds(pl.multiple_of(core * half_width + column_x * eighth, eighth), eighth)

    def at_z(offset):
        return wrap(z + offset, NZ)

    def kv_hop(hop, arriving):
        block, ahead, part = HOPS[hop]
        spot = kv.at[core, at_z(block - ahead if arriving else block), y]
        if part is not None:
            spot = spot.at[part]
        return remote(spot, spot, zas.at[hop], zar.at[hop], dp, y, at_z(ahead))

    def q_hop(hop, arriving):
        block, ahead, _ = HOPS[hop]
        spot = qf.at[core, column_x, y, at_z(block - ahead if arriving else block)]
        return remote(spot, spot, zqs.at[hop], zqr.at[hop], dp, y, at_z(ahead))

    def kv_side(block, side, arriving):
        row = y if not arriving else wrap(y - 1 if side == 0 else y + 1, NY)
        spot = kv.at[core, at_z(block), row]
        slot = BLOCKS.index(block)
        target = wrap(y + 1 if side == 0 else y - 1, NY)
        return remote(spot, spot, ys.at[side, slot], yr.at[side, slot], dp, target, z)

    def kv_pass(block, side, arriving):
        hops = 2 if arriving else 1
        row = wrap(y - hops if side == 0 else y + hops, NY)
        spot = kv.at[core, at_z(block), row, side]
        slot = BLOCKS.index(block)
        target = wrap(y + 1 if side == 0 else y - 1, NY)
        return remote(spot, spot, fs.at[side, slot], fr.at[side, slot], dp, target, z)

    def kv_swap(block, arriving):
        spot = kv.at[1 - core if arriving else core, at_z(block)]
        slot = BLOCKS.index(block)
        return remote(spot, spot, pas.at[slot], par.at[slot], partner, y, z)

    def q_side(k, arriving):
        spot = qf.at[core, column_x, wrap(y - k, NY) if arriving else y]
        return remote(spot, spot, qys.at[k - 1], qyr.at[k - 1], dp, wrap(y + k, NY), z)

    def q_cross(k, side, arriving):
        step = 1 if side == 0 else -1
        source = wrap(column_x - step, NX) if arriving else column_x
        spot = qf.at[core, source, wrap(y - k, NY)]
        target = 2 * wrap(column_x + step, NX) + core
        return remote(spot, spot, qxs.at[side, k], qxr.at[side, k], target, y, z)

    def q_pass(k, arriving):
        step = 1 if k < 2 else -1
        source = wrap(column_x - (2 * step if arriving else step), NX)
        spot = qf.at[core, source, wrap(y - k, NY)]
        target = 2 * wrap(column_x + step, NX) + core
        return remote(spot, spot, qfs.at[k], qfr.at[k], target, y, z)

    def q_swap(k, arriving):
        spot = qf.at[1 - core if arriving else core, wrap(column_x + k, NX)]
        return remote(spot, spot, pqs.at[k], pqr.at[k], partner, y, z)

    own = [
        pltpu.make_async_copy(wk.at[:, cols], kv.at[core, z, y, 0], local_sem.at[0]),
        pltpu.make_async_copy(wv.at[:, cols], kv.at[core, z, y, 1], local_sem.at[1]),
        pltpu.make_async_copy(wq.at[:, q_cols], qf.at[core, column_x, y, z], local_sem.at[2]),
    ]
    for copy in own:
        copy.start()
    greet(
        [(wrap(dp + k, groups), y, z) for k in range(1, groups)]
        + [(dp, wrap(y + k, NY), z) for k in range(1, NY)]
        + [(dp, y, wrap(z + k, NZ)) for k in FAR]
    )
    for copy in own:
        copy.wait()

    def side_out(*blocks):
        for block in blocks:
            for side in (0, 1):
                kv_side(block, side, False).start()

    def pass_on(*blocks):
        for block in blocks:
            for side in (0, 1):
                kv_side(block, side, True).wait_recv()
                kv_pass(block, side, False).start()

    def swap_out(*blocks):
        for block in blocks:
            for side in (0, 1):
                kv_pass(block, side, True).wait_recv()
            kv_swap(block, False).start()

    def go(*hops):
        for hop in hops:
            kv_hop(hop, False).start()

    def arrive(*hops):
        for hop in hops:
            kv_hop(hop, True).wait_recv()

    q_hops = tuple(hop for hop in range(len(HOPS)) if hop != 3)

    def q_go(*hops):
        for hop in hops:
            q_hop(hop, False).start()

    def q_arrive(*hops):
        for hop in hops:
            q_hop(hop, True).wait_recv()

    go(0, 1, 4, 5, 6, 7)
    side_out(0)
    q_go(0, 1, 4, 5, 6, 7)

    lane_route = jnp.broadcast_to(route[...], (groups, row_count))
    target = lax.broadcasted_iota(jnp.int32, (groups, row_count), 0)
    outgoing = jnp.where((lane_route == target) & (target != dp), 1.0, 0.0)
    before = lax.broadcasted_iota(jnp.int32, (row_count, row_count), 0)
    after = lax.broadcasted_iota(jnp.int32, (row_count, row_count), 1)
    ramp = jnp.where(before <= after, 1.0, 0.0).astype(jnp.bfloat16)
    rank = jnp.dot(outgoing.astype(jnp.bfloat16), ramp, preferred_element_type=jnp.float32)
    slot = lax.broadcasted_iota(jnp.int32, (16, row_count), 0).astype(jnp.float32) + 1.0
    picks = jnp.concatenate(
        [
            jnp.where(
                (jnp.broadcast_to(rank[g : g + 1], (16, row_count)) == slot)
                & (jnp.broadcast_to(outgoing[g : g + 1], (16, row_count)) > 0.5),
                1.0,
                0.0,
            )
            for g in range(groups)
        ],
        axis=0,
    ).astype(jnp.bfloat16)
    spread_route = jnp.broadcast_to(route[...].astype(jnp.float32), (row_count, row_count))
    column = jnp.sum(jnp.where(before == after, spread_route, 0.0), axis=1, keepdims=True)
    live = column > -0.5
    keep = column == dp.astype(jnp.float32)

    arrive(4, 5)
    side_out(-1, 1)
    arrive(0)
    go(2, 8, 9, 10)
    arrive(1)
    go(3, 11, 12, 13)
    side_out(-4, 4)
    pass_on(0)
    arrive(6, 7)
    side_out(-2, 2)
    pass_on(-1, 1)
    arrive(2, 3)
    go(14, 15)
    side_out(8)
    q_arrive(0, 1)
    q_go(2, 8, 9, 10, 11, 12, 13)
    arrive(8, 9, 11, 12)
    side_out(-5, 3, -3, 5)
    arrive(10, 13)
    side_out(-6, 6)
    pass_on(-4, 4)
    swap_out(0)
    arrive(14, 15)
    side_out(7, -7)
    q_arrive(2)
    q_go(14, 15)
    pass_on(-2, 2)
    swap_out(-1, 1)
    pass_on(8, -5)
    swap_out(-4, 4)
    pass_on(3, -3)
    swap_out(-2, 2)
    pass_on(5, -6)
    swap_out(8, -5)
    pass_on(6, 7, -7)
    q_arrive(*(hop for hop in q_hops if hop not in (0, 1, 2)))
    for k in (2, 1, 3):
        q_side(k, False).start()
    for side in (0, 1):
        q_cross(0, side, False).start()
    swap_out(3, -3, 5, -6, 6, 7, -7)

    def product(weights):
        total = None
        span = width // NY
        for line in range(NY):
            block = weights(line)
            term = jnp.dot(
                rows[:, line * span : (line + 1) * span],
                block.reshape(span, block.shape[-1]),
                preferred_element_type=jnp.float32,
            )
            total = term if total is None else total + term
        return total.astype(jnp.bfloat16)

    def swap_value(k):
        there = wrap(y + k, NY)
        return remote(out_value.at[k], in_value.at[k], vs.at[k], vr.at[k], dp, there, z)

    def swap_stat(k):
        there = wrap(y + k, NY)
        return remote(out_stat.at[k], in_stat.at[k], ss.at[k], sr.at[k], dp, there, z)

    scale = jnp.float32(1.0 / math.sqrt(head_size))
    pair = 2 * head_size
    for turn in range(NY):
        side = core if turn < 2 else 1 - core
        block = 2 * side + turn % 2
        k = wrap(block - y, NY)
        lanes = slice((turn % 2) * pair, (turn % 2 + 1) * pair)
        if turn == 1:
            for hop in (1, 3, 2):
                q_side(hop, True).wait_recv()
                for way in (0, 1):
                    q_cross(hop, way, False).start()
        if turn == 2:
            for piece_of in BLOCKS:
                kv_swap(piece_of, True).wait_recv()
        if turn == 3:
            for hop in range(NY):
                for way in (0, 1):
                    q_cross(hop, way, True).wait_recv()
            for hop in range(NY):
                q_pass(hop, False).start()
            for hop in (0, 1, 3):
                q_swap(hop, False).start()
        keys = product(lambda line: kv[side, :, line, 0, :, lanes])
        values = product(lambda line: kv[side, :, line, 1, :, lanes])
        for sub in range(2):
            span = slice(sub * head_size, (sub + 1) * head_size)
            offset = pl.multiple_of(block * pair + sub * head_size, head_size)
            scores = lax.dot_general(
                keys[:, span],
                inducing[:, pl.ds(offset, head_size)],
                (((1,), (1,)), ((), ())),
                preferred_element_type=jnp.float32,
            )
            scores = jnp.where(live, scores * scale, jnp.float32(SCORE_FLOOR))
            top = jnp.max(scores, axis=0, keepdims=True)
            terms = jnp.where(live, jnp.exp(scores - top), 0.0)
            total = jnp.sum(terms, axis=0, keepdims=True)
            weighted = lax.dot_general(
                values[:, span],
                terms.astype(jnp.bfloat16),
                (((0,), (0,)), ((), ())),
                preferred_element_type=jnp.float32,
            )
            out_value[k, sub] = weighted.astype(jnp.bfloat16)
            out_stat[k, sub] = jnp.concatenate([top, total], axis=0)

        @pl.when(k != 0)
        def _():
            swap_stat(k).start()
            swap_value(k).start()

    for k in range(NY):
        q_pass(k, True).wait_recv()
    q_swap(2, False).start()
    for k in (2, 1, 3):
        swap_stat(k).wait_recv()
        swap_value(k).wait_recv()

    for head in range(2):
        for half in range(2):
            lanes = slice(half * 128, half * 128 + 128)
            values = [out_value.at[0, head]] + [in_value.at[k, head] for k in range(1, NY)]
            stats = [out_stat.at[0, head]] + [in_stat.at[k, head] for k in range(1, NY)]
            tops = [s[0:1, lanes] for s in stats]
            totals = [s[1:2, lanes] for s in stats]
            top = tops[0]
            for other in tops[1:]:
                top = jnp.maximum(top, other)
            shares = [jnp.exp(t - top) for t in tops]
            total = totals[0] * shares[0]
            for other, share in zip(totals[1:], shares[1:]):
                total = total + other * share
            to_stat[2 * head + half] = jnp.concatenate([top, total], axis=0)
            for group in range(4):
                lines = slice(group * quarter, (group + 1) * quarter)
                value = values[0][lines, lanes].astype(jnp.float32) * shares[0]
                for source, share in zip(values[1:], shares[1:]):
                    value = value + source[lines, lanes].astype(jnp.float32) * share
                to_value[head * 8 + half * 4 + group] = value.astype(jnp.bfloat16)

    def part_stat(k):
        there = wrap(z + k, NZ)
        return remote(
            to_stat.at[lax.div(there, 4)], from_stat.at[k - 1], zss.at[k - 1], zsr.at[k - 1],
            dp, y, there,
        )

    def part_value(k):
        there = wrap(z + k, NZ)
        return remote(
            to_value.at[there], from_value.at[k - 1], zvs.at[k - 1], zvr.at[k - 1], dp, y, there
        )

    for k in ORDER:
        part_stat(k).start()
        part_value(k).start()
    for k in range(NX):
        q_swap(k, True).wait_recv()
    for block in range(NY):
        first = 2 * (block % 2)
        queries = product(
            lambda line: jnp.concatenate(
                [
                    qf[block // 2, first + e, line].reshape(width // NY, eighth)
                    for e in range(2)
                ],
                axis=1,
            )
        )
        span = slice(block * pair, (block + 1) * pair)
        local_out[:, span] = jnp.where(keep, queries.astype(jnp.float32), 0.0).astype(jnp.bfloat16)
        chosen = jnp.dot(picks, queries, preferred_element_type=jnp.float32)
        sent[:, :, span] = chosen.astype(jnp.bfloat16).reshape(groups, 16, pair)

    def move(k, arriving):
        there = wrap(dp + k, groups)
        place_at = wrap(dp - k, groups) if arriving else dp
        return remote(sent.at[there], moved.at[place_at], ms.at[k - 1], mr.at[k - 1], there, y, z)

    for k in range(1, groups):
        move(k, False).start()
    keep_own = pltpu.make_async_copy(sent.at[dp], moved.at[dp], local_sem.at[3])
    keep_own.start()

    for k in reversed(ORDER):
        part_stat(k).wait_recv()
        part_value(k).wait_recv()

    values = [to_value.at[z]] + [from_value.at[k] for k in range(NZ - 1)]
    stats = [to_stat.at[lax.div(z, 4)]] + [from_stat.at[k] for k in range(NZ - 1)]
    tops = [s[0:1, :] for s in stats]
    top = tops[0]
    for other in tops[1:]:
        top = jnp.maximum(top, other)
    value = None
    total = None
    for source, stat, own_top in zip(values, stats, tops):
        share = jnp.exp(own_top - top)
        term = source[...].astype(jnp.float32) * share
        count = stat[1:2, :] * share
        value = term if value is None else value + term
        total = count if total is None else total + count
    piece[...] = (value / total).astype(jnp.bfloat16)

    def spot(row, there):
        return summary.at[
            2 * row + lax.div(there, 8),
            pl.ds(pl.multiple_of(lax.rem(there, 4) * quarter, quarter), quarter),
            pl.ds(pl.multiple_of(lax.rem(lax.div(there, 4), 2) * 128, 128), 128),
        ]

    def spread_z(k, arriving):
        owner = wrap(z - k, NZ) if arriving else z
        return remote(
            piece, spot(y, owner), gs.at[k - 1], gr.at[k - 1], dp, y, wrap(z + k, NZ)
        )

    def spread_y(k, j, arriving):
        block = spot(wrap(y - j, NY) if arriving else y, wrap(z - k, NZ))
        source = piece if k == 0 else block
        return remote(
            source, block, hs.at[j - 1, k], hr.at[j - 1, k], dp, wrap(y + j, NY), z
        )

    for k in ORDER:
        spread_z(k, False).start()
    own_piece = pltpu.make_async_copy(piece, spot(y, z), local_sem.at[4])
    own_piece.start()
    for j in (2, 1, 3):
        spread_y(0, j, False).start()
    for k in reversed(ORDER):
        spread_z(k, True).wait_recv()
        for j in (2, 1, 3):
            spread_y(k, j, False).start()
    own_piece.wait()
    keep_own.wait()
    for k in range(NZ):
        for j in range(1, NY):
            spread_y(k, j, True).wait_recv()
    for k in range(1, groups):
        move(k, True).wait_recv()
        move(k, False).wait_send()
    for k in range(1, NY):
        swap_value(k).wait_send()
        swap_stat(k).wait_send()
    for k in range(1, NZ):
        part_value(k).wait_send()
        part_stat(k).wait_send()
        spread_z(k, False).wait_send()
    for k in range(NZ):
        for j in range(1, NY):
            spread_y(k, j, False).wait_send()

    for hop in range(len(HOPS)):
        kv_hop(hop, False).wait_send()
    for hop in q_hops:
        q_hop(hop, False).wait_send()
    for block in BLOCKS:
        for side in (0, 1):
            kv_side(block, side, False).wait_send()
            kv_pass(block, side, False).wait_send()
        kv_swap(block, False).wait_send()
    for k in range(1, NY):
        q_side(k, False).wait_send()
    for k in range(NY):
        q_pass(k, False).wait_send()
        q_swap(k, False).wait_send()
        for side in (0, 1):
            q_cross(k, side, False).wait_send()


def local(peak_rows, row_route, inducing, w_key, w_value, w_query):
    rows = peak_rows[0]
    row_count, width = rows.shape
    depth = w_key.shape[0]
    groups = lax.axis_size("dp")
    points = inducing.shape[0]
    head_size = width // HEADS
    half = width // 2
    quarter = head_size // 4
    dma = pltpu.SemaphoreType.DMA
    low, wide = jnp.bfloat16, jnp.float32
    summary, local_queries, moved = pl.pallas_call(
        kernel,
        out_shape=(
            jax.ShapeDtypeStruct((HEADS, head_size, points), low),
            jax.ShapeDtypeStruct((row_count, width), low),
            jax.ShapeDtypeStruct((groups, 16, width), low),
        ),
        in_specs=[VMEM] * 6,
        out_specs=(VMEM,) * 3,
        scratch_shapes=[
            pltpu.VMEM((2, NZ, NY, 2, depth, half), low),
            pltpu.VMEM((2, NX, NY, NZ, depth, half // NX), low),
            pltpu.VMEM((groups, 16, width), low),
            pltpu.VMEM((NY, 2, head_size, points), low),
            pltpu.VMEM((NY, 2, 2, points), wide),
            pltpu.VMEM((NY, 2, head_size, points), low),
            pltpu.VMEM((NY, 2, 2, points), wide),
            pltpu.VMEM((NZ, quarter, 128), low),
            pltpu.VMEM((4, 2, 128), wide),
            pltpu.VMEM((NZ - 1, quarter, 128), low),
            pltpu.VMEM((NZ - 1, 2, 128), wide),
            pltpu.VMEM((quarter, 128), low),
            dma((5,)),
            dma((len(HOPS),)), dma((len(HOPS),)),
            dma((len(HOPS),)), dma((len(HOPS),)),
            dma((2, NZ)), dma((2, NZ)),
            dma((2, NZ)), dma((2, NZ)),
            dma((NZ,)), dma((NZ,)),
            dma((NY - 1,)), dma((NY - 1,)),
            dma((2, NY)), dma((2, NY)),
            dma((NY,)), dma((NY,)),
            dma((NX,)), dma((NX,)),
            dma((groups - 1,)), dma((groups - 1,)),
            dma((NY,)), dma((NY,)),
            dma((NY,)), dma((NY,)),
            dma((NZ - 1,)), dma((NZ - 1,)),
            dma((NZ - 1,)), dma((NZ - 1,)),
            dma((NZ - 1,)), dma((NZ - 1,)),
            dma((NY - 1, NZ)), dma((NY - 1, NZ)),
        ],
        compiler_params=pltpu.CompilerParams(collective_id=0, has_side_effects=True),
        name="encode",
    )(rows, row_route, inducing, w_key, w_value, w_query)
    summary = summary.transpose(2, 0, 1).reshape(points, width)
    return summary[None], local_queries[None], moved.reshape(1, groups * 16, width)


def solution(mesh):
    placed = (
        P("dp", "ctx", None),
        P("dp", "ctx"),
        P(),
        P("ctx", None),
        P("ctx", None),
        P("ctx", None),
    )
    return jax.shard_map(
        local,
        mesh=mesh,
        in_specs=placed,
        out_specs=(P("dp", None, None), P("dp", "ctx", None), P("dp", "ctx", None)),
        check_vma=False,
    )
```

```python
import math

import jax
import jax.numpy as jnp
from jax import lax
from jax.experimental import pallas as pl
from jax.experimental.pallas import tpu as pltpu
from jax.sharding import PartitionSpec as P

HEADS = 8
NY = 4
NZ = 16
SCORE_FLOOR = -1e30
MESH = pl.DeviceIdType.MESH
VMEM = pl.BlockSpec(memory_space=pltpu.VMEM)

NX = 4
HOPS = (
    (0, 4, None), (0, -4, None),
    (-4, 4, 0), (4, -4, 1),
    (0, 1, None), (0, -1, None), (0, 2, None), (0, -2, None),
    (-4, 1, None), (-4, -1, None), (-4, 2, None),
    (4, 1, None), (4, -1, None), (4, -2, None),
    (8, 1, None), (8, -1, None),
)
BLOCKS = (0, -1, 1, -4, 4, -2, 2, 8, -5, 3, -3, 5, -6, 6, 7, -7)
FAR = (1, 2, 4, NZ - 4, NZ - 2, NZ - 1)
ORDER = (8, 7, 9, 6, 10, 5, 11, 4, 12, 3, 13, 2, 14, 1, 15)


def place():
    dp = lax.axis_index("dp")
    ctx = lax.axis_index("ctx")
    return dp, lax.div(ctx, NZ), lax.rem(ctx, NZ)


def wrap(value, size):
    return lax.rem(value + size, size)


def remote(src, dst, send_sem, recv_sem, dp, y, z):
    return pltpu.make_async_remote_copy(
        src_ref=src,
        dst_ref=dst,
        send_sem=send_sem,
        recv_sem=recv_sem,
        device_id=(dp, y * NZ + z),
        device_id_type=MESH,
    )


def greet(partners):
    barrier = pltpu.get_barrier_semaphore()
    for dp, y, z in partners:
        pl.semaphore_signal(barrier, inc=1, device_id=(dp, y * NZ + z), device_id_type=MESH)
    pl.semaphore_wait(barrier, len(partners))


def kernel(
    rows, route, inducing, wk, wv, wq,
    summary, local_out, moved,
    kv, qf, sent, out_value, out_stat, in_value, in_stat,
    to_value, to_stat, from_value, from_stat, piece,
    local_sem, zas, zar, zqs, zqr, ys, yr, fs, fr, xs, xr, pas, par, qys, qyr, qxs, qxr, qfs, qfr, pqs, pqr,
    ms, mr, vs, vr, ss, sr, zvs, zvr, zss, zsr, gs, gr, hs, hr,
):
    dp, y, z = place()
    core = lax.rem(dp, 2)
    partner = dp + 1 - 2 * core
    groups = moved.shape[0]
    row_count, width = rows.shape
    points = inducing.shape[0]
    head_size = width // HEADS
    half_width = width // 2
    quarter = head_size // 4
    cols = pl.ds(pl.multiple_of(core * half_width, half_width), half_width)

    column_x = lax.div(dp, 2)
    eighth = width // (2 * NX)
    q_cols = pl.ds(pl.multiple_of(core * half_width + column_x * eighth, eighth), eighth)

    def at_z(offset):
        return wrap(z + offset, NZ)

    mine = lax.rem(column_x, 2)
    strips = [slice(part * half_width // 2, (part + 1) * half_width // 2) for part in (0, 1)]

    def kv_hop(hop, arriving):
        block, ahead, part = HOPS[hop]
        spot = kv.at[core, at_z(block - ahead if arriving else block), mine, y]
        if part is not None:
            spot = spot.at[:, strips[part]]
        return remote(spot, spot, zas.at[hop], zar.at[hop], dp, y, at_z(ahead))

    def q_hop(hop, arriving):
        block, ahead, _ = HOPS[hop]
        spot = qf.at[core, column_x, y, at_z(block - ahead if arriving else block)]
        return remote(spot, spot, zqs.at[hop], zqr.at[hop], dp, y, at_z(ahead))

    def kv_side(block, side, arriving):
        row = y if not arriving else wrap(y - 1 if side == 0 else y + 1, NY)
        spot = kv.at[core, at_z(block), mine, row]
        slot = BLOCKS.index(block)
        target = wrap(y + 1 if side == 0 else y - 1, NY)
        return remote(spot, spot, ys.at[side, slot], yr.at[side, slot], dp, target, z)

    def kv_pass(block, side, arriving):
        hops = 2 if arriving else 1
        row = wrap(y - hops if side == 0 else y + hops, NY)
        spot = kv.at[core, at_z(block), mine, row, :, strips[side]]
        slot = BLOCKS.index(block)
        target = wrap(y + 1 if side == 0 else y - 1, NY)
        return remote(spot, spot, fs.at[side, slot], fr.at[side, slot], dp, target, z)

    def kv_cross(block, side, arriving):
        step = 1 if side == 0 else -1
        spot = kv.at[core, at_z(block), 1 - mine if arriving else mine, :, :, strips[side]]
        slot = BLOCKS.index(block)
        target = 2 * wrap(column_x + step, NX) + core
        return remote(spot, spot, xs.at[side, slot], xr.at[side, slot], target, y, z)

    def kv_swap(block, turn, arriving):
        matrix = mine if turn == 0 else 1 - mine
        spot = kv.at[1 - core if arriving else core, at_z(block), matrix]
        slot = BLOCKS.index(block)
        return remote(spot, spot, pas.at[turn, slot], par.at[turn, slot], partner, y, z)

    def q_side(k, arriving):
        spot = qf.at[core, column_x, wrap(y - k, NY) if arriving else y]
        return remote(spot, spot, qys.at[k - 1], qyr.at[k - 1], dp, wrap(y + k, NY), z)

    def q_cross(k, side, arriving):
        step = 1 if side == 0 else -1
        source = wrap(column_x - step, NX) if arriving else column_x
        spot = qf.at[core, source, wrap(y - k, NY)]
        target = 2 * wrap(column_x + step, NX) + core
        return remote(spot, spot, qxs.at[side, k], qxr.at[side, k], target, y, z)

    def q_pass(k, arriving):
        step = 1 if k < 2 else -1
        source = wrap(column_x - (2 * step if arriving else step), NX)
        spot = qf.at[core, source, wrap(y - k, NY)]
        target = 2 * wrap(column_x + step, NX) + core
        return remote(spot, spot, qfs.at[k], qfr.at[k], target, y, z)

    def q_swap(k, arriving):
        spot = qf.at[1 - core if arriving else core, wrap(column_x + k, NX)]
        return remote(spot, spot, pqs.at[k], pqr.at[k], partner, y, z)

    own_key, own_value, own_query = (
        pltpu.make_async_copy(wk.at[:, cols], kv.at[core, z, 0, y], local_sem.at[0]),
        pltpu.make_async_copy(wv.at[:, cols], kv.at[core, z, 1, y], local_sem.at[0]),
        pltpu.make_async_copy(wq.at[:, q_cols], qf.at[core, column_x, y, z], local_sem.at[2]),
    )

    @pl.when(mine == 0)
    def _():
        own_key.start()
        own_key.wait()

    @pl.when(mine != 0)
    def _():
        own_value.start()
        own_value.wait()

    own_query.start()
    greet(
        [(wrap(dp + k, groups), y, z) for k in range(1, groups)]
        + [(dp, wrap(y + k, NY), z) for k in range(1, NY)]
        + [(dp, y, wrap(z + k, NZ)) for k in FAR]
    )
    own_query.wait()

    def side_out(*blocks):
        for block in blocks:
            for side in (0, 1):
                kv_side(block, side, False).start()

    def pass_on(*blocks):
        for block in blocks:
            for side in (0, 1):
                kv_side(block, side, True).wait_recv()
                kv_pass(block, side, False).start()

    def swap_out(*blocks):
        for block in blocks:
            for side in (0, 1):
                kv_pass(block, side, True).wait_recv()
            for side in (0, 1):
                kv_cross(block, side, False).start()
            kv_swap(block, 0, False).start()

    def settle(*blocks):
        for block in blocks:
            for side in (0, 1):
                kv_cross(block, side, True).wait_recv()
            kv_swap(block, 1, False).start()

    def go(*hops):
        for hop in hops:
            kv_hop(hop, False).start()

    def arrive(*hops):
        for hop in hops:
            kv_hop(hop, True).wait_recv()

    q_hops = tuple(hop for hop in range(len(HOPS)) if hop != 3)

    def q_go(*hops):
        for hop in hops:
            q_hop(hop, False).start()

    def q_arrive(*hops):
        for hop in hops:
            q_hop(hop, True).wait_recv()

    go(0, 1, 4, 5, 6, 7)
    side_out(0)
    q_go(0, 1, 4, 5, 6, 7)

    lane_route = jnp.broadcast_to(route[...], (groups, row_count))
    target = lax.broadcasted_iota(jnp.int32, (groups, row_count), 0)
    outgoing = jnp.where((lane_route == target) & (target != dp), 1.0, 0.0)
    before = lax.broadcasted_iota(jnp.int32, (row_count, row_count), 0)
    after = lax.broadcasted_iota(jnp.int32, (row_count, row_count), 1)
    ramp = jnp.where(before <= after, 1.0, 0.0).astype(jnp.bfloat16)
    rank = jnp.dot(outgoing.astype(jnp.bfloat16), ramp, preferred_element_type=jnp.float32)
    slot = lax.broadcasted_iota(jnp.int32, (16, row_count), 0).astype(jnp.float32) + 1.0
    picks = jnp.concatenate(
        [
            jnp.where(
                (jnp.broadcast_to(rank[g : g + 1], (16, row_count)) == slot)
                & (jnp.broadcast_to(outgoing[g : g + 1], (16, row_count)) > 0.5),
                1.0,
                0.0,
            )
            for g in range(groups)
        ],
        axis=0,
    ).astype(jnp.bfloat16)
    spread_route = jnp.broadcast_to(route[...].astype(jnp.float32), (row_count, row_count))
    column = jnp.sum(jnp.where(before == after, spread_route, 0.0), axis=1, keepdims=True)
    live = column > -0.5
    keep = column == dp.astype(jnp.float32)

    arrive(4, 5)
    side_out(-1, 1)
    arrive(0)
    go(2, 8, 9, 10)
    arrive(1)
    go(3, 11, 12, 13)
    side_out(-4, 4)
    pass_on(0)
    arrive(6, 7)
    side_out(-2, 2)
    pass_on(-1, 1)
    arrive(2, 3)
    go(14, 15)
    side_out(8)
    q_arrive(0, 1)
    q_go(2, 8, 9, 10, 11, 12, 13)
    arrive(8, 9, 11, 12)
    side_out(-5, 3, -3, 5)
    arrive(10, 13)
    side_out(-6, 6)
    pass_on(-4, 4)
    swap_out(0)
    arrive(14, 15)
    side_out(7, -7)
    q_arrive(2)
    q_go(14, 15)
    pass_on(-2, 2)
    swap_out(-1, 1)
    pass_on(8, -5)
    swap_out(-4, 4)
    pass_on(3, -3)
    swap_out(-2, 2)
    settle(0, -1, 1)
    pass_on(5, -6)
    swap_out(8, -5)
    settle(-4, 4)
    pass_on(6, 7, -7)
    swap_out(3, -3, 5)
    settle(-2, 2, 8, -5)
    swap_out(-6, 6, 7, -7)
    settle(3, -3, 5)
    q_arrive(*(hop for hop in q_hops if hop not in (0, 1, 2)))
    for k in (2, 1, 3):
        q_side(k, False).start()
    for side in (0, 1):
        q_cross(0, side, False).start()
    settle(-6, 6, 7, -7)

    def product(weights):
        total = None
        span = width // NY
        for line in range(NY):
            block = weights(line)
            term = jnp.dot(
                rows[:, line * span : (line + 1) * span],
                block.reshape(span, block.shape[-1]),
                preferred_element_type=jnp.float32,
            )
            total = term if total is None else total + term
        return total.astype(jnp.bfloat16)

    def swap_value(k):
        there = wrap(y + k, NY)
        return remote(out_value.at[k], in_value.at[k], vs.at[k], vr.at[k], dp, there, z)

    def swap_stat(k):
        there = wrap(y + k, NY)
        return remote(out_stat.at[k], in_stat.at[k], ss.at[k], sr.at[k], dp, there, z)

    scale = jnp.float32(1.0 / math.sqrt(head_size))
    pair = 2 * head_size
    for turn in range(NY):
        side = core if turn < 2 else 1 - core
        block = 2 * side + turn % 2
        k = wrap(block - y, NY)
        lanes = slice((turn % 2) * pair, (turn % 2 + 1) * pair)
        if turn == 1:
            for hop in (1, 3, 2):
                q_side(hop, True).wait_recv()
                for way in (0, 1):
                    q_cross(hop, way, False).start()
        if turn == 2:
            for piece_of in BLOCKS:
                for part in (0, 1):
                    kv_swap(piece_of, part, True).wait_recv()
        if turn == 3:
            for hop in range(NY):
                for way in (0, 1):
                    q_cross(hop, way, True).wait_recv()
            for hop in range(NY):
                q_pass(hop, False).start()
            for hop in (0, 1, 3):
                q_swap(hop, False).start()
        keys = product(lambda line: kv[side, :, 0, line, :, lanes])
        values = product(lambda line: kv[side, :, 1, line, :, lanes])
        for sub in range(2):
            span = slice(sub * head_size, (sub + 1) * head_size)
            offset = pl.multiple_of(block * pair + sub * head_size, head_size)
            scores = lax.dot_general(
                keys[:, span],
                inducing[:, pl.ds(offset, head_size)],
                (((1,), (1,)), ((), ())),
                preferred_element_type=jnp.float32,
            )
            scores = jnp.where(live, scores * scale, jnp.float32(SCORE_FLOOR))
            top = jnp.max(scores, axis=0, keepdims=True)
            terms = jnp.where(live, jnp.exp(scores - top), 0.0)
            total = jnp.sum(terms, axis=0, keepdims=True)
            weighted = lax.dot_general(
                values[:, span],
                terms.astype(jnp.bfloat16),
                (((0,), (0,)), ((), ())),
                preferred_element_type=jnp.float32,
            )
            out_value[k, sub] = weighted.astype(jnp.bfloat16)
            out_stat[k, sub] = jnp.concatenate([top, total], axis=0)

        @pl.when(k != 0)
        def _():
            swap_stat(k).start()
            swap_value(k).start()

    for k in range(NY):
        q_pass(k, True).wait_recv()
    q_swap(2, False).start()
    for k in (2, 1, 3):
        swap_stat(k).wait_recv()
        swap_value(k).wait_recv()

    for head in range(2):
        for half in range(2):
            lanes = slice(half * 128, half * 128 + 128)
            values = [out_value.at[0, head]] + [in_value.at[k, head] for k in range(1, NY)]
            stats = [out_stat.at[0, head]] + [in_stat.at[k, head] for k in range(1, NY)]
            tops = [s[0:1, lanes] for s in stats]
            totals = [s[1:2, lanes] for s in stats]
            top = tops[0]
            for other in tops[1:]:
                top = jnp.maximum(top, other)
            shares = [jnp.exp(t - top) for t in tops]
            total = totals[0] * shares[0]
            for other, share in zip(totals[1:], shares[1:]):
                total = total + other * share
            to_stat[2 * head + half] = jnp.concatenate([top, total], axis=0)
            for group in range(4):
                lines = slice(group * quarter, (group + 1) * quarter)
                value = values[0][lines, lanes].astype(jnp.float32) * shares[0]
                for source, share in zip(values[1:], shares[1:]):
                    value = value + source[lines, lanes].astype(jnp.float32) * share
                to_value[head * 8 + half * 4 + group] = value.astype(jnp.bfloat16)

    def part_stat(k):
        there = wrap(z + k, NZ)
        return remote(
            to_stat.at[lax.div(there, 4)], from_stat.at[k - 1], zss.at[k - 1], zsr.at[k - 1],
            dp, y, there,
        )

    def part_value(k):
        there = wrap(z + k, NZ)
        return remote(
            to_value.at[there], from_value.at[k - 1], zvs.at[k - 1], zvr.at[k - 1], dp, y, there
        )

    for k in ORDER:
        part_stat(k).start()
        part_value(k).start()
    for k in range(NX):
        q_swap(k, True).wait_recv()
    for block in range(NY):
        first = 2 * (block % 2)
        queries = product(
            lambda line: jnp.concatenate(
                [
                    qf[block // 2, first + e, line].reshape(width // NY, eighth)
                    for e in range(2)
                ],
                axis=1,
            )
        )
        span = slice(block * pair, (block + 1) * pair)
        local_out[:, span] = jnp.where(keep, queries.astype(jnp.float32), 0.0).astype(jnp.bfloat16)
        chosen = jnp.dot(picks, queries, preferred_element_type=jnp.float32)
        sent[:, :, span] = chosen.astype(jnp.bfloat16).reshape(groups, 16, pair)

    def move(k, arriving):
        there = wrap(dp + k, groups)
        place_at = wrap(dp - k, groups) if arriving else dp
        return remote(sent.at[there], moved.at[place_at], ms.at[k - 1], mr.at[k - 1], there, y, z)

    for k in range(1, groups):
        move(k, False).start()
    keep_own = pltpu.make_async_copy(sent.at[dp], moved.at[dp], local_sem.at[3])
    keep_own.start()

    for k in reversed(ORDER):
        part_stat(k).wait_recv()
        part_value(k).wait_recv()

    values = [to_value.at[z]] + [from_value.at[k] for k in range(NZ - 1)]
    stats = [to_stat.at[lax.div(z, 4)]] + [from_stat.at[k] for k in range(NZ - 1)]
    tops = [s[0:1, :] for s in stats]
    top = tops[0]
    for other in tops[1:]:
        top = jnp.maximum(top, other)
    value = None
    total = None
    for source, stat, own_top in zip(values, stats, tops):
        share = jnp.exp(own_top - top)
        term = source[...].astype(jnp.float32) * share
        count = stat[1:2, :] * share
        value = term if value is None else value + term
        total = count if total is None else total + count
    piece[...] = (value / total).astype(jnp.bfloat16)

    def spot(row, there):
        return summary.at[
            2 * row + lax.div(there, 8),
            pl.ds(pl.multiple_of(lax.rem(there, 4) * quarter, quarter), quarter),
            pl.ds(pl.multiple_of(lax.rem(lax.div(there, 4), 2) * 128, 128), 128),
        ]

    def spread_z(k, arriving):
        owner = wrap(z - k, NZ) if arriving else z
        return remote(
            piece, spot(y, owner), gs.at[k - 1], gr.at[k - 1], dp, y, wrap(z + k, NZ)
        )

    def spread_y(k, j, arriving):
        block = spot(wrap(y - j, NY) if arriving else y, wrap(z - k, NZ))
        source = piece if k == 0 else block
        return remote(
            source, block, hs.at[j - 1, k], hr.at[j - 1, k], dp, wrap(y + j, NY), z
        )

    for k in ORDER:
        spread_z(k, False).start()
    own_piece = pltpu.make_async_copy(piece, spot(y, z), local_sem.at[4])
    own_piece.start()
    for j in (2, 1, 3):
        spread_y(0, j, False).start()
    for k in reversed(ORDER):
        spread_z(k, True).wait_recv()
        for j in (2, 1, 3):
            spread_y(k, j, False).start()
    own_piece.wait()
    keep_own.wait()
    for k in range(NZ):
        for j in range(1, NY):
            spread_y(k, j, True).wait_recv()
    for k in range(1, groups):
        move(k, True).wait_recv()
        move(k, False).wait_send()
    for k in range(1, NY):
        swap_value(k).wait_send()
        swap_stat(k).wait_send()
    for k in range(1, NZ):
        part_value(k).wait_send()
        part_stat(k).wait_send()
        spread_z(k, False).wait_send()
    for k in range(NZ):
        for j in range(1, NY):
            spread_y(k, j, False).wait_send()

    for hop in range(len(HOPS)):
        kv_hop(hop, False).wait_send()
    for hop in q_hops:
        q_hop(hop, False).wait_send()
    for block in BLOCKS:
        for side in (0, 1):
            kv_side(block, side, False).wait_send()
            kv_pass(block, side, False).wait_send()
            kv_cross(block, side, False).wait_send()
            kv_swap(block, side, False).wait_send()
    for k in range(1, NY):
        q_side(k, False).wait_send()
    for k in range(NY):
        q_pass(k, False).wait_send()
        q_swap(k, False).wait_send()
        for side in (0, 1):
            q_cross(k, side, False).wait_send()


def local(peak_rows, row_route, inducing, w_key, w_value, w_query):
    rows = peak_rows[0]
    row_count, width = rows.shape
    depth = w_key.shape[0]
    groups = lax.axis_size("dp")
    points = inducing.shape[0]
    head_size = width // HEADS
    half = width // 2
    quarter = head_size // 4
    dma = pltpu.SemaphoreType.DMA
    low, wide = jnp.bfloat16, jnp.float32
    summary, local_queries, moved = pl.pallas_call(
        kernel,
        out_shape=(
            jax.ShapeDtypeStruct((HEADS, head_size, points), low),
            jax.ShapeDtypeStruct((row_count, width), low),
            jax.ShapeDtypeStruct((groups, 16, width), low),
        ),
        in_specs=[VMEM] * 6,
        out_specs=(VMEM,) * 3,
        scratch_shapes=[
            pltpu.VMEM((2, NZ, 2, NY, depth, half), low),
            pltpu.VMEM((2, NX, NY, NZ, depth, half // NX), low),
            pltpu.VMEM((groups, 16, width), low),
            pltpu.VMEM((NY, 2, head_size, points), low),
            pltpu.VMEM((NY, 2, 2, points), wide),
            pltpu.VMEM((NY, 2, head_size, points), low),
            pltpu.VMEM((NY, 2, 2, points), wide),
            pltpu.VMEM((NZ, quarter, 128), low),
            pltpu.VMEM((4, 2, 128), wide),
            pltpu.VMEM((NZ - 1, quarter, 128), low),
            pltpu.VMEM((NZ - 1, 2, 128), wide),
            pltpu.VMEM((quarter, 128), low),
            dma((5,)),
            dma((len(HOPS),)), dma((len(HOPS),)),
            dma((len(HOPS),)), dma((len(HOPS),)),
            dma((2, NZ)), dma((2, NZ)),
            dma((2, NZ)), dma((2, NZ)),
            dma((2, NZ)), dma((2, NZ)),
            dma((2, NZ)), dma((2, NZ)),
            dma((NY - 1,)), dma((NY - 1,)),
            dma((2, NY)), dma((2, NY)),
            dma((NY,)), dma((NY,)),
            dma((NX,)), dma((NX,)),
            dma((groups - 1,)), dma((groups - 1,)),
            dma((NY,)), dma((NY,)),
            dma((NY,)), dma((NY,)),
            dma((NZ - 1,)), dma((NZ - 1,)),
            dma((NZ - 1,)), dma((NZ - 1,)),
            dma((NZ - 1,)), dma((NZ - 1,)),
            dma((NY - 1, NZ)), dma((NY - 1, NZ)),
        ],
        compiler_params=pltpu.CompilerParams(collective_id=0, has_side_effects=True),
        name="encode",
    )(rows, row_route, inducing, w_key, w_value, w_query)
    summary = summary.transpose(2, 0, 1).reshape(points, width)
    return summary[None], local_queries[None], moved.reshape(1, groups * 16, width)


def solution(mesh):
    placed = (
        P("dp", "ctx", None),
        P("dp", "ctx"),
        P(),
        P("ctx", None),
        P("ctx", None),
        P("ctx", None),
    )
    return jax.shard_map(
        local,
        mesh=mesh,
        in_specs=placed,
        out_specs=(P("dp", None, None), P("dp", "ctx", None), P("dp", "ctx", None)),
        check_vma=False,
    )
```

```python
import math

import jax
import jax.numpy as jnp
from jax import lax
from jax.experimental import pallas as pl
from jax.experimental.pallas import tpu as pltpu
from jax.sharding import PartitionSpec as P

HEADS = 8
NY = 4
NZ = 16
SCORE_FLOOR = -1e30
MESH = pl.DeviceIdType.MESH
VMEM = pl.BlockSpec(memory_space=pltpu.VMEM)

NX = 4
HOPS = (
    (0, 4, None), (0, -4, None),
    (-4, 4, 0), (4, -4, 1),
    (0, 1, None), (0, -1, None), (0, 2, None), (0, -2, None),
    (-4, 1, None), (-4, -1, None), (-4, 2, None),
    (4, 1, None), (4, -1, None), (4, -2, None),
    (8, 1, None), (8, -1, None),
)
BLOCKS = (0, -1, 1, -4, 4, -2, 2, 8, -5, 3, -3, 5, -6, 6, 7, -7)
LATE = (-6, 6, 7, -7)
FAR = (1, 2, 4, NZ - 4, NZ - 2, NZ - 1)
ORDER = (8, 7, 9, 6, 10, 5, 11, 4, 12, 3, 13, 2, 14, 1, 15)


def place():
    dp = lax.axis_index("dp")
    ctx = lax.axis_index("ctx")
    return dp, lax.div(ctx, NZ), lax.rem(ctx, NZ)


def wrap(value, size):
    return lax.rem(value + size, size)


def remote(src, dst, send_sem, recv_sem, dp, y, z):
    return pltpu.make_async_remote_copy(
        src_ref=src,
        dst_ref=dst,
        send_sem=send_sem,
        recv_sem=recv_sem,
        device_id=(dp, y * NZ + z),
        device_id_type=MESH,
    )


def greet(partners):
    barrier = pltpu.get_barrier_semaphore()
    for dp, y, z in partners:
        pl.semaphore_signal(barrier, inc=1, device_id=(dp, y * NZ + z), device_id_type=MESH)
    pl.semaphore_wait(barrier, len(partners))


def kernel(
    rows, route, inducing, wk, wv, wq,
    summary, local_out, moved,
    kv, qf, sent, out_value, out_stat, in_value, in_stat,
    to_value, to_stat, from_value, from_stat, piece,
    local_sem, zas, zar, zqs, zqr, ys, yr, fs, fr, pas, par, qys, qyr, qxs, qxr, qfs, qfr, pqs, pqr,
    ms, mr, vs, vr, ss, sr, zvs, zvr, zss, zsr, gs, gr, hs, hr,
):
    dp, y, z = place()
    core = lax.rem(dp, 2)
    partner = dp + 1 - 2 * core
    groups = moved.shape[0]
    row_count, width = rows.shape
    points = inducing.shape[0]
    head_size = width // HEADS
    half_width = width // 2
    quarter = head_size // 4
    cols = pl.ds(pl.multiple_of(core * half_width, half_width), half_width)

    column_x = lax.div(dp, 2)
    eighth = width // (2 * NX)
    q_cols = pl.ds(pl.multiple_of(core * half_width + column_x * eighth, eighth), eighth)

    def at_z(offset):
        return wrap(z + offset, NZ)

    def kv_hop(hop, arriving):
        block, ahead, part = HOPS[hop]
        spot = kv.at[core, at_z(block - ahead if arriving else block), y]
        if part is not None:
            spot = spot.at[part]
        return remote(spot, spot, zas.at[hop], zar.at[hop], dp, y, at_z(ahead))

    def q_hop(hop, arriving):
        block, ahead, _ = HOPS[hop]
        spot = qf.at[core, column_x, y, at_z(block - ahead if arriving else block)]
        return remote(spot, spot, zqs.at[hop], zqr.at[hop], dp, y, at_z(ahead))

    def kv_side(block, side, arriving):
        row = y if not arriving else wrap(y - 1 if side == 0 else y + 1, NY)
        spot = kv.at[core, at_z(block), row]
        slot = BLOCKS.index(block)
        target = wrap(y + 1 if side == 0 else y - 1, NY)
        return remote(spot, spot, ys.at[side, slot], yr.at[side, slot], dp, target, z)

    def kv_pass(block, side, arriving):
        hops = 2 if arriving else 1
        row = wrap(y - hops if side == 0 else y + hops, NY)
        spot = kv.at[core, at_z(block), row, side]
        slot = BLOCKS.index(block)
        target = wrap(y + 1 if side == 0 else y - 1, NY)
        return remote(spot, spot, fs.at[side, slot], fr.at[side, slot], dp, target, z)

    def kv_direct(block, arriving):
        spot = kv.at[core, at_z(block), wrap(y + 2, NY) if arriving else y]
        slot = BLOCKS.index(block)
        target = wrap(y + 2, NY)
        return remote(spot, spot, fs.at[0, slot], fr.at[0, slot], dp, target, z)

    def kv_swap(block, arriving):
        spot = kv.at[1 - core if arriving else core, at_z(block)]
        slot = BLOCKS.index(block)
        return remote(spot, spot, pas.at[slot], par.at[slot], partner, y, z)

    def q_side(k, arriving):
        spot = qf.at[core, column_x, wrap(y - k, NY) if arriving else y]
        return remote(spot, spot, qys.at[k - 1], qyr.at[k - 1], dp, wrap(y + k, NY), z)

    def q_cross(k, side, arriving):
        step = 1 if side == 0 else -1
        source = wrap(column_x - step, NX) if arriving else column_x
        spot = qf.at[core, source, wrap(y - k, NY)]
        target = 2 * wrap(column_x + step, NX) + core
        return remote(spot, spot, qxs.at[side, k], qxr.at[side, k], target, y, z)

    def q_pass(k, arriving):
        step = 1 if k < 2 else -1
        source = wrap(column_x - (2 * step if arriving else step), NX)
        spot = qf.at[core, source, wrap(y - k, NY)]
        target = 2 * wrap(column_x + step, NX) + core
        return remote(spot, spot, qfs.at[k], qfr.at[k], target, y, z)

    def q_swap(k, arriving):
        spot = qf.at[1 - core if arriving else core, wrap(column_x + k, NX)]
        return remote(spot, spot, pqs.at[k], pqr.at[k], partner, y, z)

    own = [
        pltpu.make_async_copy(wk.at[:, cols], kv.at[core, z, y, 0], local_sem.at[0]),
        pltpu.make_async_copy(wv.at[:, cols], kv.at[core, z, y, 1], local_sem.at[1]),
        pltpu.make_async_copy(wq.at[:, q_cols], qf.at[core, column_x, y, z], local_sem.at[2]),
    ]
    for copy in own:
        copy.start()
    greet(
        [(wrap(dp + k, groups), y, z) for k in range(1, groups)]
        + [(dp, wrap(y + k, NY), z) for k in range(1, NY)]
        + [(dp, y, wrap(z + k, NZ)) for k in FAR]
    )
    for copy in own:
        copy.wait()

    def side_out(*blocks):
        for block in blocks:
            for side in (0, 1):
                kv_side(block, side, False).start()
            if block in LATE:
                kv_direct(block, False).start()

    def pass_on(*blocks):
        for block in blocks:
            for side in (0, 1):
                kv_side(block, side, True).wait_recv()
                if block not in LATE:
                    kv_pass(block, side, False).start()

    def swap_out(*blocks):
        for block in blocks:
            if block in LATE:
                kv_direct(block, True).wait_recv()
            else:
                for side in (0, 1):
                    kv_pass(block, side, True).wait_recv()
            kv_swap(block, False).start()

    def go(*hops):
        for hop in hops:
            kv_hop(hop, False).start()

    def arrive(*hops):
        for hop in hops:
            kv_hop(hop, True).wait_recv()

    q_hops = tuple(hop for hop in range(len(HOPS)) if hop != 3)

    def q_go(*hops):
        for hop in hops:
            q_hop(hop, False).start()

    def q_arrive(*hops):
        for hop in hops:
            q_hop(hop, True).wait_recv()

    go(0, 1, 4, 5, 6, 7)
    side_out(0)
    q_go(0, 1, 4, 5, 6, 7)

    lane_route = jnp.broadcast_to(route[...], (groups, row_count))
    target = lax.broadcasted_iota(jnp.int32, (groups, row_count), 0)
    outgoing = jnp.where((lane_route == target) & (target != dp), 1.0, 0.0)
    before = lax.broadcasted_iota(jnp.int32, (row_count, row_count), 0)
    after = lax.broadcasted_iota(jnp.int32, (row_count, row_count), 1)
    ramp = jnp.where(before <= after, 1.0, 0.0).astype(jnp.bfloat16)
    rank = jnp.dot(outgoing.astype(jnp.bfloat16), ramp, preferred_element_type=jnp.float32)
    slot = lax.broadcasted_iota(jnp.int32, (16, row_count), 0).astype(jnp.float32) + 1.0
    picks = jnp.concatenate(
        [
            jnp.where(
                (jnp.broadcast_to(rank[g : g + 1], (16, row_count)) == slot)
                & (jnp.broadcast_to(outgoing[g : g + 1], (16, row_count)) > 0.5),
                1.0,
                0.0,
            )
            for g in range(groups)
        ],
        axis=0,
    ).astype(jnp.bfloat16)
    spread_route = jnp.broadcast_to(route[...].astype(jnp.float32), (row_count, row_count))
    column = jnp.sum(jnp.where(before == after, spread_route, 0.0), axis=1, keepdims=True)
    live = column > -0.5
    keep = column == dp.astype(jnp.float32)

    arrive(4, 5)
    side_out(-1, 1)
    arrive(0)
    go(2, 8, 9, 10)
    arrive(1)
    go(3, 11, 12, 13)
    side_out(-4, 4)
    pass_on(0)
    arrive(6, 7)
    side_out(-2, 2)
    pass_on(-1, 1)
    arrive(2, 3)
    go(14, 15)
    side_out(8)
    q_arrive(0, 1)
    q_go(2, 8, 9, 10, 11, 12, 13)
    arrive(8, 9, 11, 12)
    side_out(-5, 3, -3, 5)
    arrive(10, 13)
    side_out(-6, 6)
    pass_on(-4, 4)
    swap_out(0)
    arrive(14, 15)
    side_out(7, -7)
    q_arrive(2)
    q_go(14, 15)
    pass_on(-2, 2)
    swap_out(-1, 1)
    pass_on(8, -5)
    swap_out(-4, 4)
    pass_on(3, -3)
    swap_out(-2, 2)
    pass_on(5, -6)
    swap_out(8, -5)
    pass_on(6, 7, -7)
    q_arrive(*(hop for hop in q_hops if hop not in (0, 1, 2)))
    for k in (2, 1, 3):
        q_side(k, False).start()
    for side in (0, 1):
        q_cross(0, side, False).start()
    swap_out(3, -3, 5, -6, 6, 7, -7)

    def product(weights):
        total = None
        span = width // NY
        for line in range(NY):
            block = weights(line)
            term = jnp.dot(
                rows[:, line * span : (line + 1) * span],
                block.reshape(span, block.shape[-1]),
                preferred_element_type=jnp.float32,
            )
            total = term if total is None else total + term
        return total.astype(jnp.bfloat16)

    def swap_value(k):
        there = wrap(y + k, NY)
        return remote(out_value.at[k], in_value.at[k], vs.at[k], vr.at[k], dp, there, z)

    def swap_stat(k):
        there = wrap(y + k, NY)
        return remote(out_stat.at[k], in_stat.at[k], ss.at[k], sr.at[k], dp, there, z)

    scale = jnp.float32(1.0 / math.sqrt(head_size))
    pair = 2 * head_size
    for turn in range(NY):
        side = core if turn < 2 else 1 - core
        block = 2 * side + turn % 2
        k = wrap(block - y, NY)
        lanes = slice((turn % 2) * pair, (turn % 2 + 1) * pair)
        if turn == 1:
            for hop in (1, 3, 2):
                q_side(hop, True).wait_recv()
                for way in (0, 1):
                    q_cross(hop, way, False).start()
        if turn == 2:
            for piece_of in BLOCKS:
                kv_swap(piece_of, True).wait_recv()
        if turn == 3:
            for hop in range(NY):
                for way in (0, 1):
                    q_cross(hop, way, True).wait_recv()
            for hop in range(NY):
                q_pass(hop, False).start()
            for hop in (0, 1, 3):
                q_swap(hop, False).start()
        keys = product(lambda line: kv[side, :, line, 0, :, lanes])
        values = product(lambda line: kv[side, :, line, 1, :, lanes])
        for sub in range(2):
            span = slice(sub * head_size, (sub + 1) * head_size)
            offset = pl.multiple_of(block * pair + sub * head_size, head_size)
            scores = lax.dot_general(
                keys[:, span],
                inducing[:, pl.ds(offset, head_size)],
                (((1,), (1,)), ((), ())),
                preferred_element_type=jnp.float32,
            )
            scores = jnp.where(live, scores * scale, jnp.float32(SCORE_FLOOR))
            top = jnp.max(scores, axis=0, keepdims=True)
            terms = jnp.where(live, jnp.exp(scores - top), 0.0)
            total = jnp.sum(terms, axis=0, keepdims=True)
            weighted = lax.dot_general(
                values[:, span],
                terms.astype(jnp.bfloat16),
                (((0,), (0,)), ((), ())),
                preferred_element_type=jnp.float32,
            )
            out_value[k, sub] = weighted.astype(jnp.bfloat16)
            out_stat[k, sub] = jnp.concatenate([top, total], axis=0)

        @pl.when(k != 0)
        def _():
            swap_stat(k).start()
            swap_value(k).start()

    for k in range(NY):
        q_pass(k, True).wait_recv()
    q_swap(2, False).start()
    for k in (2, 1, 3):
        swap_stat(k).wait_recv()
        swap_value(k).wait_recv()

    def part_stat(k):
        there = wrap(z + k, NZ)
        return remote(
            to_stat.at[lax.div(there, 4)], from_stat.at[k - 1], zss.at[k - 1], zsr.at[k - 1],
            dp, y, there,
        )

    def part_value(k):
        there = wrap(z + k, NZ)
        return remote(
            to_value.at[there], from_value.at[k - 1], zvs.at[k - 1], zvr.at[k - 1], dp, y, there
        )

    for turn in (2, 1, 3, 0):
        spot_of = lax.rem(lax.div(z, 4) + turn, 4)
        head = lax.div(spot_of, 2)
        lanes = pl.ds(pl.multiple_of(lax.rem(spot_of, 2) * 128, 128), 128)
        values = [out_value.at[0, head]] + [in_value.at[k, head] for k in range(1, NY)]
        stats = [out_stat.at[0, head]] + [in_stat.at[k, head] for k in range(1, NY)]
        tops = [s[0:1, lanes] for s in stats]
        totals = [s[1:2, lanes] for s in stats]
        top = tops[0]
        for other in tops[1:]:
            top = jnp.maximum(top, other)
        shares = [jnp.exp(t - top) for t in tops]
        total = totals[0] * shares[0]
        for other, share in zip(totals[1:], shares[1:]):
            total = total + other * share
        to_stat[spot_of] = jnp.concatenate([top, total], axis=0)
        for group in range(4):
            lines = slice(group * quarter, (group + 1) * quarter)
            value = values[0][lines, lanes].astype(jnp.float32) * shares[0]
            for source, share in zip(values[1:], shares[1:]):
                value = value + source[lines, lanes].astype(jnp.float32) * share
            to_value[spot_of * 4 + group] = value.astype(jnp.bfloat16)
        for group in range(4):
            k = wrap(spot_of * 4 + group - z, NZ)

            @pl.when(k != 0)
            def _(k=k):
                part_stat(k).start()
                part_value(k).start()

    for k in range(NX):
        q_swap(k, True).wait_recv()
    for block in range(NY):
        first = 2 * (block % 2)
        queries = product(
            lambda line: jnp.concatenate(
                [
                    qf[block // 2, first + e, line].reshape(width // NY, eighth)
                    for e in range(2)
                ],
                axis=1,
            )
        )
        span = slice(block * pair, (block + 1) * pair)
        local_out[:, span] = jnp.where(keep, queries.astype(jnp.float32), 0.0).astype(jnp.bfloat16)
        chosen = jnp.dot(picks, queries, preferred_element_type=jnp.float32)
        sent[:, :, span] = chosen.astype(jnp.bfloat16).reshape(groups, 16, pair)

    def move(k, arriving):
        there = wrap(dp + k, groups)
        place_at = wrap(dp - k, groups) if arriving else dp
        return remote(sent.at[there], moved.at[place_at], ms.at[k - 1], mr.at[k - 1], there, y, z)

    for k in range(1, groups):
        move(k, False).start()
    keep_own = pltpu.make_async_copy(sent.at[dp], moved.at[dp], local_sem.at[3])
    keep_own.start()

    for k in reversed(ORDER):
        part_stat(k).wait_recv()
        part_value(k).wait_recv()

    values = [to_value.at[z]] + [from_value.at[k] for k in range(NZ - 1)]
    stats = [to_stat.at[lax.div(z, 4)]] + [from_stat.at[k] for k in range(NZ - 1)]
    tops = [s[0:1, :] for s in stats]
    top = tops[0]
    for other in tops[1:]:
        top = jnp.maximum(top, other)
    value = None
    total = None
    for source, stat, own_top in zip(values, stats, tops):
        share = jnp.exp(own_top - top)
        term = source[...].astype(jnp.float32) * share
        count = stat[1:2, :] * share
        value = term if value is None else value + term
        total = count if total is None else total + count
    piece[...] = (value / total).astype(jnp.bfloat16)

    def spot(row, there):
        return summary.at[
            2 * row + lax.div(there, 8),
            pl.ds(pl.multiple_of(lax.rem(there, 4) * quarter, quarter), quarter),
            pl.ds(pl.multiple_of(lax.rem(lax.div(there, 4), 2) * 128, 128), 128),
        ]

    def spread_z(k, arriving):
        owner = wrap(z - k, NZ) if arriving else z
        return remote(
            piece, spot(y, owner), gs.at[k - 1], gr.at[k - 1], dp, y, wrap(z + k, NZ)
        )

    def spread_y(k, j, arriving):
        block = spot(wrap(y - j, NY) if arriving else y, wrap(z - k, NZ))
        source = piece if k == 0 else block
        return remote(
            source, block, hs.at[j - 1, k], hr.at[j - 1, k], dp, wrap(y + j, NY), z
        )

    for k in ORDER:
        spread_z(k, False).start()
    own_piece = pltpu.make_async_copy(piece, spot(y, z), local_sem.at[4])
    own_piece.start()
    for j in (2, 1, 3):
        spread_y(0, j, False).start()
    for k in reversed(ORDER):
        spread_z(k, True).wait_recv()
        for j in (2, 1, 3):
            spread_y(k, j, False).start()
    own_piece.wait()
    keep_own.wait()
    for k in range(NZ):
        for j in range(1, NY):
            spread_y(k, j, True).wait_recv()
    for k in range(1, groups):
        move(k, True).wait_recv()
        move(k, False).wait_send()
    for k in range(1, NY):
        swap_value(k).wait_send()
        swap_stat(k).wait_send()
    for k in range(1, NZ):
        part_value(k).wait_send()
        part_stat(k).wait_send()
        spread_z(k, False).wait_send()
    for k in range(NZ):
        for j in range(1, NY):
            spread_y(k, j, False).wait_send()

    for hop in range(len(HOPS)):
        kv_hop(hop, False).wait_send()
    for hop in q_hops:
        q_hop(hop, False).wait_send()
    for block in BLOCKS:
        for side in (0, 1):
            kv_side(block, side, False).wait_send()
            if block not in LATE:
                kv_pass(block, side, False).wait_send()
        if block in LATE:
            kv_direct(block, False).wait_send()
        kv_swap(block, False).wait_send()
    for k in range(1, NY):
        q_side(k, False).wait_send()
    for k in range(NY):
        q_pass(k, False).wait_send()
        q_swap(k, False).wait_send()
        for side in (0, 1):
            q_cross(k, side, False).wait_send()


def local(peak_rows, row_route, inducing, w_key, w_value, w_query):
    rows = peak_rows[0]
    row_count, width = rows.shape
    depth = w_key.shape[0]
    groups = lax.axis_size("dp")
    points = inducing.shape[0]
    head_size = width // HEADS
    half = width // 2
    quarter = head_size // 4
    dma = pltpu.SemaphoreType.DMA
    low, wide = jnp.bfloat16, jnp.float32
    summary, local_queries, moved = pl.pallas_call(
        kernel,
        out_shape=(
            jax.ShapeDtypeStruct((HEADS, head_size, points), low),
            jax.ShapeDtypeStruct((row_count, width), low),
            jax.ShapeDtypeStruct((groups, 16, width), low),
        ),
        in_specs=[VMEM] * 6,
        out_specs=(VMEM,) * 3,
        scratch_shapes=[
            pltpu.VMEM((2, NZ, NY, 2, depth, half), low),
            pltpu.VMEM((2, NX, NY, NZ, depth, half // NX), low),
            pltpu.VMEM((groups, 16, width), low),
            pltpu.VMEM((NY, 2, head_size, points), low),
            pltpu.VMEM((NY, 2, 2, points), wide),
            pltpu.VMEM((NY, 2, head_size, points), low),
            pltpu.VMEM((NY, 2, 2, points), wide),
            pltpu.VMEM((NZ, quarter, 128), low),
            pltpu.VMEM((4, 2, 128), wide),
            pltpu.VMEM((NZ - 1, quarter, 128), low),
            pltpu.VMEM((NZ - 1, 2, 128), wide),
            pltpu.VMEM((quarter, 128), low),
            dma((5,)),
            dma((len(HOPS),)), dma((len(HOPS),)),
            dma((len(HOPS),)), dma((len(HOPS),)),
            dma((2, NZ)), dma((2, NZ)),
            dma((2, NZ)), dma((2, NZ)),
            dma((NZ,)), dma((NZ,)),
            dma((NY - 1,)), dma((NY - 1,)),
            dma((2, NY)), dma((2, NY)),
            dma((NY,)), dma((NY,)),
            dma((NX,)), dma((NX,)),
            dma((groups - 1,)), dma((groups - 1,)),
            dma((NY,)), dma((NY,)),
            dma((NY,)), dma((NY,)),
            dma((NZ - 1,)), dma((NZ - 1,)),
            dma((NZ - 1,)), dma((NZ - 1,)),
            dma((NZ - 1,)), dma((NZ - 1,)),
            dma((NY - 1, NZ)), dma((NY - 1, NZ)),
        ],
        compiler_params=pltpu.CompilerParams(collective_id=0, has_side_effects=True),
        name="encode",
    )(rows, row_route, inducing, w_key, w_value, w_query)
    summary = summary.transpose(2, 0, 1).reshape(points, width)
    return summary[None], local_queries[None], moved.reshape(1, groups * 16, width)


def solution(mesh):
    placed = (
        P("dp", "ctx", None),
        P("dp", "ctx"),
        P(),
        P("ctx", None),
        P("ctx", None),
        P("ctx", None),
    )
    return jax.shard_map(
        local,
        mesh=mesh,
        in_specs=placed,
        out_specs=(P("dp", None, None), P("dp", "ctx", None), P("dp", "ctx", None)),
        check_vma=False,
    )
```
